128 devices in a mesh: gx: 8 (over x, core), gz: 16 (over y, z).
Axes of the slice: x: 4, y: 4, z: 4, core: 2. Of those that a mesh axis runs over, the one named last changes fastest.
Arguments:
- velocity: float32 [3, 2048, 8, 2048], P(None, 'gx', None, 'gz'), may hold values from -32 to 32
Outputs:
- grad_x: float32 [3, 2048, 8, 2048], P(None, 'gx', None, 'gz')
- grad_z: float32 [3, 2048, 8, 2048], P(None, 'gx', None, 'gz')
- convect: float32 [3, 2048, 8, 2048], P(None, 'gx', None, 'gz')
- rebuilt: float32 [2, 2048, 8, 2048], P(None, 'gx', None, 'gz')
The draws below stay inside these ranges and needn't reach their ends.
All inputs are finite; a program needn't handle non-finite values.
Results may differ from the reference program's by a relative error of at most 0.0003.
Values sent between devices are 32-bit elements; how exact they have to be, the bound alone decides.
No kernel may reach another device: no remote copies, remote signals or barrier semaphores. Data moves between devices by JAX's collectives and lax.ppermute only.
A program may use at most 256 MiB of HBM per device.

```python
import math
import jax
import jax.numpy as jnp
from jax import lax

NX = 2048
NZ = 2048
Y = 8


def draw_velocity(key, part):
    noise_key, xrough_key, zrough_key = jax.random.split(jax.random.fold_in(key, 17), 3)
    x_frac = jnp.arange(NX, dtype=jnp.float32) / NX
    z_frac = jnp.arange(NZ, dtype=jnp.float32) / NZ
    rough_x = jax.random.uniform(xrough_key, (3, NX), jnp.float32, -0.35, 0.35)
    rough_z = jax.random.uniform(zrough_key, (3, NZ), jnp.float32, -0.35, 0.35)
    growth = math.log(3.0)
    noise = jax.random.truncated_normal(noise_key, -4.0, 4.0, (3, NX, Y, NZ), jnp.float32)
    norm_factor = growth / (math.exp(growth) - 1.0)
    scale_x = jnp.exp(growth * x_frac[None, :] + rough_x) * norm_factor
    scale_z = jnp.exp(growth * z_frac[None, :] + rough_z) * norm_factor
    value = noise * scale_x[:, :, None, None] * scale_z[:, None, None, :]
    return value


def setup_inputs(seed: int = 0) -> dict:
    key_of = jax.random.split(jax.random.key(seed), 2)
    velocity = draw_velocity(jax.random.fold_in(key_of[1], 71), 0)
    return dict(velocity=velocity)


ALPHA = 1.0 / 3.0
COEF_A = 14.0 / 9.0
COEF_B = 1.0 / 9.0

def derivative(field, axis_at):
    length = field.shape[axis_at]
    spectrum = jnp.fft.rfft(field, axis=axis_at)
    wave = 2.0 * math.pi * jnp.arange(length // 2 + 1).astype(field.dtype) / length
    factor = (COEF_A * jnp.sin(wave) + 0.5 * COEF_B * jnp.sin(2.0 * wave)) / (1.0 + 2.0 * ALPHA * jnp.cos(wave))
    shape_list = [1] * field.ndim
    shape_list[axis_at] = length // 2 + 1
    result = jnp.fft.irfft(spectrum * (1j * factor.reshape(shape_list)), n=length, axis=axis_at)
    return result.astype(field.dtype)

def primitive(values, axis_at):
    length = values.shape[axis_at]
    shape_list = [1] * values.ndim
    shape_list[axis_at] = length
    position = jnp.arange(length).astype(values.dtype).reshape(shape_list)
    mean_value = lax.optimization_barrier(jnp.mean(values, axis=axis_at, keepdims=True))
    centred_sum = lax.optimization_barrier(jnp.sum(values * (position - 0.5 * (length - 1)), axis=axis_at, keepdims=True))
    running = jnp.cumsum(values, axis=axis_at)
    zero_slice = jnp.zeros_like(lax.slice_in_dim(values, 0, 1, axis=axis_at))
    before = jnp.concatenate([zero_slice, lax.slice_in_dim(running, 0, length - 1, axis=axis_at)], axis_at)
    result = before - position * mean_value + 0.5 * (values - mean_value) + centred_sum / length
    return -result / math.sqrt(length)

def reference(velocity):
    along_x = []
    along_z = []
    fluxes = []
    for comp in range(3):
        field = velocity[comp]
        along_x.append(derivative(field, 0))
        along_z.append(derivative(field, 2))
        flux_x = velocity[0] * field
        flux_z = velocity[2] * field
        fluxes.append(derivative(flux_x, 0) + derivative(flux_z, 2))
    rebuilt = jnp.stack([primitive(along_z[2], 0), primitive(along_x[0], 2)])
    return (jnp.stack(along_x), jnp.stack(along_z), jnp.stack(fluxes), rebuilt)
```

```python
import math

import jax
import jax.numpy as jnp
import numpy as np
from jax import lax
from jax.experimental import pallas as pl
from jax.experimental.pallas import tpu as pltpu
from jax.sharding import PartitionSpec as P

ALPHA = 1.0 / 3.0
COEF_A = 14.0 / 9.0
COEF_B = 1.0 / 9.0
LANES = 128
F32 = jnp.float32
BF16 = jnp.bfloat16

RHO = (-1.0 + math.sqrt(1.0 - 4.0 * ALPHA * ALPHA)) / (2.0 * ALPHA)


def kernel_weights():
    reach = 400
    k = np.arange(-reach, reach + 1)
    green = RHO ** np.abs(k).astype(np.float64) / math.sqrt(1.0 - 4.0 * ALPHA * ALPHA)

    def shifted(s):
        out = np.zeros_like(green)
        if s >= 0:
            out[s:] = green[: len(green) - s]
        else:
            out[:s] = green[-s:]
        return out

    direct = 0.5 * COEF_A * (shifted(-1) - shifted(1)) + 0.25 * COEF_B * (shifted(-2) - shifted(2))
    total = np.concatenate([[0.0], np.cumsum(direct)])
    return {m: total[m + reach] for m in range(-2, 4)}


_W = kernel_weights()
NEAR = _W[1]
TAIL = _W[2] / RHO**2
KAPPA = TAIL * RHO * RHO
REACH = 96


def h_of(m):
    m = np.asarray(m)
    m = np.where(m <= 0, 1 - m, m)
    return np.where(m == 1, NEAR, TAIL * RHO ** m.astype(np.float64))


def split_np(x):
    hi = x.astype(BF16)
    lo = (x - hi.astype(np.float64)).astype(BF16)
    return hi, lo


def going_up(length):
    j = np.arange(length)
    w = (RHO - 1.0) * RHO ** (length - j).astype(np.float64)
    w[-1] = RHO**2
    return w


def going_down(length):
    return going_up(length)[::-1] * -1.0


def z_matrices():
    j = np.arange(LANES)
    inner = h_of(j[None, :] - j[:, None])
    inner[LANES - 1] = 0.0
    inner_hi, inner_lo = split_np(inner)
    rim = np.stack(
        [
            h_of(j + 1),
            TAIL * RHO ** j.astype(np.float64),
            h_of(LANES - j),
            TAIL * RHO ** (LANES - 1 - j).astype(np.float64),
        ]
    )
    rim_hi, rim_lo = split_np(rim)
    pad = np.zeros((LANES - 12, LANES), BF16)
    first = np.concatenate([inner_hi, inner_hi], 0)
    second = np.concatenate([inner_lo, rim_hi, rim_hi, rim_lo, pad], 0)
    return np.stack([first, second])


def sum_matrices():
    j = np.arange(LANES)
    lower = (j[:, None] < j[None, :]) + 0.5 * (j[:, None] == j[None, :])
    ones = np.ones((3, LANES))
    slope = -np.broadcast_to(j, (3, LANES))
    pad = np.zeros((LANES - 6, LANES))
    first = np.concatenate([lower, lower], 0)
    second = np.concatenate([lower, ones, slope, pad], 0)
    return np.stack([first, second]).astype(BF16)


def split2(x):
    hi = x.astype(BF16)
    return hi, (x - hi.astype(F32)).astype(BF16)


def split3(x):
    hi = x.astype(BF16)
    rest = x - hi.astype(F32)
    mid = rest.astype(BF16)
    return hi, mid, (rest - mid.astype(F32)).astype(BF16)


def dot(a, b):
    return lax.dot_general(a, b, (((1,), (0,)), ((), ())), preferred_element_type=F32)


def product(values, name):
    out = values[name[0]]
    for c in name[1:]:
        out = out * values[c]
    return out


COMP = {"u": 0, "v": 1, "w": 2}


def edges_call(velocity, x_sums, x_cells, z_sums, z_cells):
    comps, nx, ny, nz = velocity.shape
    step = 32
    steps = nx // step
    reach = min(REACH // step, steps)
    sub = LANES // ny
    chunks = nx // sub
    per = step // sub
    names_x = sorted(set("".join(x_sums + x_cells)))
    names_z = sorted(set("".join(z_sums + z_cells)))
    nqx = len(x_sums) + len(x_cells)
    nqz = len(z_sums) + len(z_cells)
    up_x = going_up(nx)
    down_x = going_down(nx)
    cut = min(REACH, nz)

    def body(v_ref, w_ref, xu_ref, xd_ref, zu_ref, zd_ref):
        i = pl.program_id(0)

        def x_part(ref, weights, rows_of, cell_at, start):
            for blk, at in rows_of:

                @pl.when(i == at)
                def _(blk=blk, at=at):
                    for q, name in enumerate(x_sums):
                        acc = None
                        for k in range(step):
                            vals = {c: v_ref[COMP[c], k] for c in set(name)}
                            term = product(vals, name) * np.float32(weights[at * step + k])
                            acc = term if acc is None else acc + term
                        if at == start:
                            ref[q] = acc
                        else:
                            ref[q] = ref[q] + acc
                    if at * step <= cell_at < (at + 1) * step:
                        for q, name in enumerate(x_cells):
                            ref[len(x_sums) + q] = v_ref[COMP[name], cell_at - at * step]

        ups = list(range(steps - reach, steps))
        downs = list(range(reach))
        x_part(xu_ref, up_x, list(enumerate(ups)), nx - 1, ups[0])
        x_part(xd_ref, down_x, list(enumerate(downs)), 0, downs[0])

        for s in range(per):
            at = i * per + s
            t = {}
            for c in names_z:
                t[c] = v_ref[COMP[c], s * sub : (s + 1) * sub].reshape(LANES, nz).T
            for q, name in enumerate(z_sums):
                f = product(t, name)
                up = jnp.sum(f[nz - cut :] * w_ref[0, nz - cut :], axis=0, keepdims=True)
                down = jnp.sum(f[:cut] * w_ref[1, :cut], axis=0, keepdims=True)
                zu_ref[q, pl.ds(at, 1), :] = up
                zd_ref[q, pl.ds(at, 1), :] = down
            for q, name in enumerate(z_cells):
                zu_ref[len(z_sums) + q, pl.ds(at, 1), :] = t[name][nz - 1 : nz]
                zd_ref[len(z_sums) + q, pl.ds(at, 1), :] = t[name][0:1]

    weights = np.stack([going_up(nz), going_down(nz)]).astype(np.float32)
    weights = jnp.asarray(np.broadcast_to(weights[:, :, None], (2, nz, LANES)))
    xs = jax.ShapeDtypeStruct((nqx, ny, nz), F32)
    zs = jax.ShapeDtypeStruct((nqz, chunks, LANES), F32)
    xspec = pl.BlockSpec(xs.shape, lambda i: (0, 0, 0))
    zspec = pl.BlockSpec(zs.shape, lambda i: (0, 0, 0))
    return pl.pallas_call(
        body,
        grid=(steps,),
        in_specs=[
            pl.BlockSpec((comps, step, ny, nz), lambda i: (0, i, 0, 0)),
            pl.BlockSpec(weights.shape, lambda i: (0, 0, 0)),
        ],
        out_specs=[xspec, xspec, zspec, zspec],
        out_shape=[xs, xs, zs, zs],
        name="edges",
        cost_estimate=pl.CostEstimate(
            flops=40 * len(z_sums) * nx * ny * nz, transcendentals=0, bytes_accessed=4 * comps * nx * ny * nz
        ),
    )(velocity, weights)


def x_derivative(read, write, scratch, nx, sum_before, cell_before, sum_after, cell_after):
    unroll = 8
    blocks = nx // unroll

    def forward(b, carry):
        state, before, here = carry
        base = b * unroll
        for k in range(unroll):
            i = base + k
            if k == unroll - 1:
                nxt = jnp.where(b == blocks - 1, cell_after, read(jnp.minimum(i + 1, nx - 1)))
            else:
                nxt = read(i + 1)
            scratch[i] = state + NEAR * (nxt - before)
            state = RHO * state + KAPPA * (here - before)
            before, here = here, nxt
        return state, before, here

    lax.fori_loop(0, blocks, forward, (TAIL * sum_before, cell_before, read(0)))

    def backward(b, carry):
        state, after = carry
        base = (blocks - 1 - b) * unroll
        for k in reversed(range(unroll)):
            i = base + k
            here = read(i)
            write(i, scratch[i] + state)
            state = RHO * state + KAPPA * (after - here)
            after = here
        return state, after

    lax.fori_loop(0, blocks, backward, (TAIL * sum_after, cell_after))


def rim_rows(scratch, sum_before, cell_before, first, last, sum_after, cell_after):
    terms = [first - cell_before, sum_before, cell_after - last, sum_after]
    for q, term in enumerate(terms):
        hi = term.astype(BF16).astype(F32)
        lo = (term - hi).astype(BF16).astype(F32)
        scratch[:, q, :] = hi
        scratch[:, 4 + q, :] = lo
        scratch[:, 8 + q, :] = hi


def z_derivative(read, write, rim, mats, chunks, together=2):
    lane = lax.broadcasted_iota(jnp.int32, (LANES, LANES), 1)
    keep = lane < LANES - 1

    def step(b, _):
        his, los, rims = [], [], []
        for k in range(together):
            c = b * together + k
            f = read(c)
            e = jnp.where(keep, pltpu.roll(f, LANES - 1, 1) - f, 0.0)
            hi, lo = split2(e)
            his.append(hi)
            los.append(lo)
            rims.append(rim[c].T.astype(BF16))
        hi = jnp.concatenate(his, 0)
        lo = jnp.concatenate(los, 0)
        st = jnp.concatenate(rims, 0)
        g = dot(jnp.concatenate([hi, lo], 1), mats[0]) + dot(jnp.concatenate([hi, st], 1), mats[1])
        for k in range(together):
            write(b * together + k, g[k * LANES : (k + 1) * LANES])
        return 0

    lax.fori_loop(0, chunks // together, step, 0)


def whole(shape):
    return pl.BlockSpec(shape, lambda *_: (0,) * len(shape))


def comp_spec(shape, at):
    return pl.BlockSpec((None,) + tuple(shape[1:]), lambda *g: (at(*g), 0, 0, 0))


def params():
    return pltpu.CompilerParams(vmem_limit_bytes=40 * 2**20)


def cost(fields, size):
    return pl.CostEstimate(flops=fields * size * 512, transcendentals=0, bytes_accessed=fields * size * 8)


def slopes_first(velocity, x_halo, z_halo, mats):
    _, nx, ny, nz = velocity.shape
    sub = LANES // ny
    chunks = nx // sub

    def body(u_ref, w_ref, xl, xr, zl, zr, zown_l, zown_r, m_ref, gx, gz, sx, sz, scratch, rim):
        rim[...] = jnp.zeros_like(rim)
        rim_rows(rim, zl[0], zl[1], zown_l[1], zown_r[1], zr[0], zr[1])

        def read(c):
            return w_ref[pl.ds(c * sub, sub)].reshape(LANES, nz)

        def write(c, g):
            gz[pl.ds(c * sub, sub)] = g.reshape(sub, ny, nz)

        z_derivative(read, write, rim, m_ref, chunks)

        def write_x(i, g):
            gx[i] = g

        x_derivative(lambda i: u_ref[i], write_x, scratch, nx, xl[0], xl[1], xr[0], xr[1])

        def add(b, carry):
            total, moment = carry
            for k in range(8):
                g = gz[b * 8 + k]
                at = (b * 8 + k).astype(F32) - 0.5 * (nx - 1)
                total = total + g
                moment = moment + at * g
            return total, moment

        zero = jnp.zeros((ny, nz), F32)
        total, moment = lax.fori_loop(0, nx // 8, add, (zero, zero))
        sx[0] = total
        sx[1] = moment

        at = lax.broadcasted_iota(jnp.int32, (nz, LANES), 0).astype(F32) - 0.5 * (nz - 1)
        for c in range(chunks):
            t = gx[c * sub : (c + 1) * sub].reshape(LANES, nz).T
            sz[0, c : c + 1, :] = jnp.sum(t, axis=0, keepdims=True)
            sz[1, c : c + 1, :] = jnp.sum(t * at, axis=0, keepdims=True)

    full = jax.ShapeDtypeStruct(velocity.shape, F32)
    sx = jax.ShapeDtypeStruct((2, ny, nz), F32)
    sz = jax.ShapeDtypeStruct((2, chunks, LANES), F32)
    small = [*x_halo, *z_halo, mats]
    return pl.pallas_call(
        body,
        grid=(1,),
        in_specs=[comp_spec(velocity.shape, lambda i: 0), comp_spec(velocity.shape, lambda i: 2)]
        + [whole(a.shape) for a in small],
        out_specs=[
            comp_spec(velocity.shape, lambda i: 0),
            comp_spec(velocity.shape, lambda i: 2),
            whole(sx.shape),
            whole(sz.shape),
        ],
        out_shape=[full, full, sx, sz],
        scratch_shapes=[pltpu.VMEM((nx, ny, nz), F32), pltpu.VMEM((chunks, LANES, LANES), F32)],
        compiler_params=params(),
        name="slopes_first",
        cost_estimate=cost(2, nx * ny * nz),
    )(velocity, velocity, *small)


def slopes_x(velocity, x_halo, gx):
    _, nx, ny, nz = velocity.shape

    def body(f_ref, xl, xr, _, out, scratch):
        c = pl.program_id(0)

        def write(i, g):
            out[i] = g

        x_derivative(
            lambda i: f_ref[i], write, scratch, nx, xl[c], xl[6 + c], xr[c], xr[6 + c]
        )

    return pl.pallas_call(
        body,
        grid=(2,),
        in_specs=[comp_spec(velocity.shape, lambda c: c + 1)]
        + [whole(a.shape) for a in x_halo]
        + [pl.BlockSpec(memory_space=pl.ANY)],
        out_specs=comp_spec(velocity.shape, lambda c: c + 1),
        out_shape=jax.ShapeDtypeStruct(velocity.shape, F32),
        scratch_shapes=[pltpu.VMEM((nx, ny, nz), F32)],
        input_output_aliases={3: 0},
        compiler_params=params(),
        name="slopes_x",
        cost_estimate=cost(2, nx * ny * nz),
    )(velocity, *x_halo, gx)


def slopes_z(velocity, z_halo, mats, gz):
    _, nx, ny, nz = velocity.shape
    sub = LANES // ny
    chunks = nx // sub

    def body(f_ref, zl, zr, zown_l, zown_r, m_ref, _, out, rim):
        c = pl.program_id(0)

        @pl.when(c == 0)
        def _():
            rim[...] = jnp.zeros_like(rim)

        rim_rows(rim, zl[c], zl[5 + c], zown_l[5 + c], zown_r[5 + c], zr[c], zr[5 + c])

        def read(k):
            return f_ref[pl.ds(k * sub, sub)].reshape(LANES, nz)

        def write(k, g):
            out[pl.ds(k * sub, sub)] = g.reshape(sub, ny, nz)

        z_derivative(read, write, rim, m_ref, chunks)

    return pl.pallas_call(
        body,
        grid=(2,),
        in_specs=[comp_spec(velocity.shape, lambda c: c)]
        + [whole(a.shape) for a in (*z_halo, mats)]
        + [pl.BlockSpec(memory_space=pl.ANY)],
        out_specs=comp_spec(velocity.shape, lambda c: c),
        out_shape=jax.ShapeDtypeStruct(velocity.shape, F32),
        scratch_shapes=[pltpu.VMEM((chunks, LANES, LANES), F32)],
        input_output_aliases={6: 0},
        compiler_params=params(),
        name="slopes_z",
        cost_estimate=cost(2, nx * ny * nz),
    )(velocity, *z_halo, mats, gz)


def divergence(velocity, x_halo, z_halo, mats):
    _, nx, ny, nz = velocity.shape
    sub = LANES // ny
    chunks = nx // sub

    def body(f_ref, u_ref, w_ref, xl, xr, zl, zr, zown_l, zown_r, m_ref, out, scratch, rim):
        c = pl.program_id(0)

        @pl.when(c == 0)
        def _():
            rim[...] = jnp.zeros_like(rim)

        rim_rows(
            rim,
            zl[2 + c],
            zl[7] * zl[5 + c],
            zown_l[7] * zown_l[5 + c],
            zown_r[7] * zown_r[5 + c],
            zr[2 + c],
            zr[7] * zr[5 + c],
        )

        def read(k):
            at = pl.ds(k * sub, sub)
            return (w_ref[at] * f_ref[at]).reshape(LANES, nz)

        def write(k, g):
            out[pl.ds(k * sub, sub)] = g.reshape(sub, ny, nz)

        z_derivative(read, write, rim, m_ref, chunks)

        def write_x(i, g):
            out[i] = out[i] + g

        x_derivative(
            lambda i: u_ref[i] * f_ref[i],
            write_x,
            scratch,
            nx,
            xl[2 + c],
            xl[5] * xl[5 + c],
            xr[2 + c],
            xr[5] * xr[5 + c],
        )

    return pl.pallas_call(
        body,
        grid=(3,),
        in_specs=[
            comp_spec(velocity.shape, lambda c: c),
            comp_spec(velocity.shape, lambda c: 0),
            comp_spec(velocity.shape, lambda c: 2),
        ]
        + [whole(a.shape) for a in (*x_halo, *z_halo, mats)],
        out_specs=comp_spec(velocity.shape, lambda c: c),
        out_shape=jax.ShapeDtypeStruct(velocity.shape, F32),
        scratch_shapes=[pltpu.VMEM((nx, ny, nz), F32), pltpu.VMEM((chunks, LANES, LANES), F32)],
        compiler_params=params(),
        name="divergence",
        cost_estimate=cost(6, nx * ny * nz),
    )(velocity, velocity, velocity, *x_halo, *z_halo, mats)


def rebuild(gx, gz, x_terms, z_terms, mats, total_x, total_z):
    _, nx, ny, nz = gx.shape
    sub = LANES // ny
    chunks = nx // sub
    scale_x = -1.0 / math.sqrt(total_x)
    scale_z = -1.0 / math.sqrt(total_z)

    def body(u_ref, w_ref, xt, zt, m_ref, out, rim):
        rim[...] = jnp.zeros_like(rim)
        for q in range(2):
            for p, part in enumerate(split3(zt[q])):
                rim[:, 3 * q + p, :] = part.astype(F32)

        mean = xt[1]

        def along_x(b, acc):
            for k in range(8):
                i = b * 8 + k
                g = w_ref[i]
                out[0, i] = scale_x * (acc + 0.5 * g)
                acc = acc + (g - mean)
            return acc

        lax.fori_loop(0, nx // 8, along_x, xt[0])

        def along_z(b, _):
            for k in range(2):
                c = b * 2 + k
                at = pl.ds(c * sub, sub)
                hi, mid, lo = split3(u_ref[at].reshape(LANES, nz))
                st = rim[c].T.astype(BF16)
                g = dot(jnp.concatenate([hi, mid], 1), m_ref[0]) + dot(
                    jnp.concatenate([lo, st], 1), m_ref[1]
                )
                out[1, at] = (scale_z * g).reshape(sub, ny, nz)
            return 0

        lax.fori_loop(0, chunks // 2, along_z, 0)

    small = (x_terms, z_terms, mats)
    shape = (2,) + gx.shape[1:]
    return pl.pallas_call(
        body,
        grid=(1,),
        in_specs=[comp_spec(gx.shape, lambda i: 0), comp_spec(gx.shape, lambda i: 2)]
        + [whole(a.shape) for a in small],
        out_specs=whole(shape),
        out_shape=jax.ShapeDtypeStruct(shape, F32),
        scratch_shapes=[pltpu.VMEM((chunks, LANES, LANES), F32)],
        compiler_params=params(),
        name="rebuild",
        cost_estimate=cost(2, nx * ny * nz),
    )(gx, gz, *small)


def swap(array, axis, up, down):
    n = lax.axis_size(axis)
    before = lax.ppermute(up, axis, [(i, (i + 1) % n) for i in range(n)])
    after = lax.ppermute(down, axis, [((i + 1) % n, i) for i in range(n)])
    return before, after


def level(axis, terms, count, stride):
    n = lax.axis_size(axis)
    mine = (lax.axis_index(axis) // stride) % count
    parts = []
    for k in range(1, count):
        pairs = []
        for i in range(n):
            own = (i // stride) % count
            pairs.append((i, i + ((own + k) % count - own) * stride))
        parts.append(((mine - k) % count < mine, lax.ppermute(terms, axis, pairs)))
    return parts


def combine(terms, before, parts):
    for lower, part in parts:
        before = before + jnp.where(lower, part[0], 0.0)
        terms = terms + part
    return terms, before


def line_terms(terms, before, start, total_len):
    mean = terms[0] / total_len
    offset = before - (start + 0.5) * mean + terms[1] / total_len
    return jnp.stack([offset, mean])


def body(velocity):
    _, nx, ny, nz = velocity.shape
    size_x = lax.axis_size("gx")
    size_z = lax.axis_size("gz")
    total_x = nx * size_x
    total_z = nz * size_z
    mats = jnp.asarray(z_matrices())
    sums = jnp.asarray(sum_matrices())

    xu, xd, zu, zd = edges_call(velocity, ["u"], ["u"], ["w"], ["w"])
    x_first = swap(None, "gx", xu, xd)
    z_first = swap(None, "gz", zu, zd)
    xu2, xd2, zu2, zd2 = edges_call(
        velocity,
        ["v", "w", "uu", "uv", "uw"],
        ["u", "v", "w"],
        ["u", "v", "wu", "wv", "ww"],
        ["u", "v", "w"],
    )
    x_rest = swap(None, "gx", xu2, xd2)
    z_rest = (*swap(None, "gz", zu2, zd2), zd2, zu2)

    gx, gz, sx, sz = slopes_first(velocity, x_first, (*z_first, zd, zu), mats)

    x0 = (lax.axis_index("gx") * nx).astype(F32)
    z0 = (lax.axis_index("gz") * nz).astype(F32)
    centre_x = x0 + (0.5 * (nx - 1) - 0.5 * (total_x - 1))
    centre_z = z0 + (0.5 * (nz - 1) - 0.5 * (total_z - 1))
    tx = jnp.stack([sx[0], sx[1] + centre_x * sx[0]])
    tz = jnp.stack([sz[0], sz[1] + centre_z * sz[0]])

    px = level("gx", tx, 2, 1)
    pz = level("gz", tz, 4, 1)
    gx = slopes_x(velocity, x_rest, gx)
    gz = slopes_z(velocity, z_rest, mats, gz)
    tx, bx = combine(tx, 0.0, px)
    tz, bz = combine(tz, 0.0, pz)
    px = level("gx", tx, size_x // 2, 2)
    pz = level("gz", tz, size_z // 4, 4)
    convect = divergence(velocity, x_rest, z_rest, mats)
    tx, bx = combine(tx, bx, px)
    tz, bz = combine(tz, bz, pz)
    rebuilt = rebuild(
        gx,
        gz,
        line_terms(tx, bx, x0, total_x),
        line_terms(tz, bz, z0, total_z),
        sums,
        total_x,
        total_z,
    )
    return (gx, gz, convect, rebuilt)


def solution(mesh):
    spec = P(None, "gx", None, "gz")
    return jax.shard_map(
        body, mesh=mesh, in_specs=(spec,), out_specs=(spec,) * 4, check_vma=False
    )
```

```python
import math

import jax
import jax.numpy as jnp
import numpy as np
from jax import lax
from jax.experimental import pallas as pl
from jax.experimental.pallas import tpu as pltpu
from jax.sharding import PartitionSpec as P

ALPHA = 1.0 / 3.0
COEF_A = 14.0 / 9.0
COEF_B = 1.0 / 9.0
LANES = 128
F32 = jnp.float32
VMEM = pl.BlockSpec(memory_space=pltpu.VMEM)
HBM = pl.BlockSpec(memory_space=pltpu.HBM)
ANY = pl.BlockSpec(memory_space=pl.ANY)
BF16 = jnp.bfloat16

RHO = (-1.0 + math.sqrt(1.0 - 4.0 * ALPHA * ALPHA)) / (2.0 * ALPHA)


def kernel_weights():
    reach = 400
    k = np.arange(-reach, reach + 1)
    green = RHO ** np.abs(k).astype(np.float64) / math.sqrt(1.0 - 4.0 * ALPHA * ALPHA)

    def shifted(s):
        out = np.zeros_like(green)
        if s >= 0:
            out[s:] = green[: len(green) - s]
        else:
            out[:s] = green[-s:]
        return out

    direct = 0.5 * COEF_A * (shifted(-1) - shifted(1)) + 0.25 * COEF_B * (shifted(-2) - shifted(2))
    total = np.concatenate([[0.0], np.cumsum(direct)])
    return {m: total[m + reach] for m in range(-2, 4)}


_W = kernel_weights()
NEAR = _W[1]
TAIL = _W[2] / RHO**2
KAPPA = TAIL * RHO * RHO
TOGETHER = 16
REACH = 96


def h_of(m):
    m = np.asarray(m)
    m = np.where(m <= 0, 1 - m, m)
    return np.where(m == 1, NEAR, TAIL * RHO ** m.astype(np.float64))


def split_np(x):
    hi = x.astype(BF16)
    lo = (x - hi.astype(np.float64)).astype(BF16)
    return hi, lo


def going_up(length):
    j = np.arange(length)
    w = (RHO - 1.0) * RHO ** (length - j).astype(np.float64)
    w[-1] = RHO**2
    return w


def going_down(length):
    return going_up(length)[::-1] * -1.0


def z_inner():
    j = np.arange(LANES)
    inner = h_of(j[None, :] - j[:, None])
    inner[LANES - 1] = 0.0
    hi, lo = split_np(inner)
    return np.stack([hi, lo])


def z_rims(fields):
    j = np.arange(LANES)
    rim = np.stack(
        [
            h_of(j + 1),
            TAIL * RHO ** j.astype(np.float64),
            h_of(LANES - j),
            TAIL * RHO ** (LANES - 1 - j).astype(np.float64),
        ]
    )
    hi, lo = split_np(rim)
    out = np.zeros((fields, LANES, LANES), BF16)
    for f in range(fields):
        out[f, 12 * f : 12 * f + 12] = np.concatenate([hi, hi, lo], 0)
    return out


def sum_matrices():
    j = np.arange(LANES)
    lower = (j[:, None] < j[None, :]) + 0.5 * (j[:, None] == j[None, :])
    ones = np.ones((3, LANES))
    slope = -np.broadcast_to(j, (3, LANES))
    pad = np.zeros((LANES - 6, LANES))
    first = np.concatenate([lower, lower], 0)
    second = np.concatenate([lower, ones, slope, pad], 0)
    return np.stack([first, second]).astype(BF16)


def split2(x):
    hi = x.astype(BF16)
    return hi, (x - hi.astype(F32)).astype(BF16)


def split3(x):
    hi = x.astype(BF16)
    rest = x - hi.astype(F32)
    mid = rest.astype(BF16)
    return hi, mid, (rest - mid.astype(F32)).astype(BF16)


def dot(a, b):
    return lax.dot_general(a, b, (((1,), (0,)), ((), ())), preferred_element_type=F32)


def product(values, name):
    out = values[name[0]]
    for c in name[1:]:
        out = out * values[c]
    return out


COMP = {"u": 0, "v": 1, "w": 2}


X_SUMS = ["u", "v", "w", "uu", "uv", "uw"]
Z_SUMS = ["u", "v", "w", "wu", "wv", "ww"]
CELLS = ["u", "v", "w"]


def edges_call(velocity):
    comps, nx, ny, nz = velocity.shape
    sub = LANES // ny
    chunks = nx // sub
    nq = len(X_SUMS) + len(CELLS)
    up_x = going_up(nx)
    down_x = going_down(nx)
    cut_x = min(REACH, nx)
    cut = min(REACH, nz)
    group = 8
    parts = 4
    part = nx // parts
    first_up = nx - cut_x

    def ramp(powers, factor):
        row = lax.broadcasted_iota(jnp.int32, (8, LANES), 0)
        tile = jnp.zeros((8, LANES), F32)
        for k in range(8):
            tile = jnp.where(row == k, np.float32(powers[k]), tile)
        return [tile * np.float32(f) for f in factor]

    def z_weights():
        up = going_up(nz)[nz - cut :]
        down = going_down(nz)[:cut]
        tiles = cut // 8
        ups = ramp(up[:8] / up[0], up[::8])
        downs = ramp(down[-8:] / down[-8], down[::8])
        row = lax.broadcasted_iota(jnp.int32, (8, LANES), 0)
        ups[-1] = jnp.where(row == 7, np.float32(up[-1]), ups[-1])
        downs[0] = ramp(down[8:16] / down[8], [down[8] / RHO**8])[0]
        downs[0] = jnp.where(row == 0, np.float32(down[0]), downs[0])
        return jnp.concatenate(ups, 0), jnp.concatenate(downs, 0)

    def body(v_hbm, xu_ref, xd_ref, zu_ref, zd_ref, v_ref, sems):
        copies = [
            pltpu.make_async_copy(
                v_hbm.at[:, pl.ds(p * part, part)], v_ref.at[:, pl.ds(p * part, part)], sems.at[p]
            )
            for p in range(parts)
        ]
        for copy in copies:
            copy.start()
        weight_up, weight_down = z_weights()

        def x_rows(acc, weights, rows):
            for i in rows:
                vals = {c: v_ref[COMP[c], i] for c in CELLS}
                for q, name in enumerate(X_SUMS):
                    term = product(vals, name) * np.float32(weights[i])
                    acc[q] = term if acc[q] is None else acc[q] + term

        ups = [None] * len(X_SUMS)
        downs = [None] * len(X_SUMS)
        rows_z = {}
        for p in range(parts):
            copies[p].wait()
            for s in range(p * part // sub, (p + 1) * part // sub):
                t = {c: v_ref[COMP[c], s * sub : (s + 1) * sub].reshape(LANES, nz).T for c in CELLS}
                for q, name in enumerate(Z_SUMS):
                    f = product(t, name)
                    up = jnp.sum(f[nz - cut :] * weight_up, axis=0, keepdims=True)
                    down = jnp.sum(f[:cut] * weight_down, axis=0, keepdims=True)
                    rows_z.setdefault(q, []).append((up, down))
                for q, name in enumerate(CELLS):
                    rows_z.setdefault(len(Z_SUMS) + q, []).append((t[name][nz - 1 : nz], t[name][0:1]))
                if (s + 1) % group == 0:
                    at = s + 1 - group
                    for q, pairs in rows_z.items():
                        zu_ref[q, at : at + group] = jnp.concatenate([r[0] for r in pairs], 0)
                        zd_ref[q, at : at + group] = jnp.concatenate([r[1] for r in pairs], 0)
                    rows_z = {}
            here = range(p * part, (p + 1) * part)
            x_rows(downs, down_x, [i for i in here if i < cut_x])
            x_rows(ups, up_x, [i for i in here if i >= first_up])
        for q in range(len(X_SUMS)):
            xu_ref[q] = ups[q]
            xd_ref[q] = downs[q]
        for q in range(len(CELLS)):
            xu_ref[len(X_SUMS) + q] = v_ref[q, nx - 1]
            xd_ref[len(X_SUMS) + q] = v_ref[q, 0]

    xs = jax.ShapeDtypeStruct((nq, ny, nz), F32)
    zs = jax.ShapeDtypeStruct((nq, chunks, LANES), F32)
    return pl.pallas_call(
        body,
        in_specs=[HBM],
        out_specs=[VMEM] * 5,
        out_shape=[xs, xs, zs, zs, jax.ShapeDtypeStruct(velocity.shape, F32)],
        scratch_shapes=[pltpu.SemaphoreType.DMA((parts,))],
        compiler_params=params(),
        name="edges",
        cost_estimate=cost(6, nx * ny * nz),
    )(pltpu.with_memory_space_constraint(velocity, pltpu.HBM))


def x_derivative(read, write, scratch, nx, sum_before, cell_before, sum_after, cell_after, done=None):
    unroll = 8
    half = nx // 2
    blocks = half // unroll
    grown = [KAPPA * RHO ** -(k + 1) for k in range(unroll)]
    power = [RHO**k for k in range(unroll + 1)]

    def sweep(first):
        def step(b, carry):
            low, before, here, high, after, there = carry
            lows = (0 if first else half) + b * unroll
            highs = (nx if first else half) - 1 - b * unroll
            for k in range(unroll):
                i = lows + k
                part = low if k == 0 else power[k] * low
                edge = here - before
                if first:
                    nxt = read(i + 1)
                    scratch[i] = part
                else:
                    if k == unroll - 1:
                        nxt = jnp.where(b == blocks - 1, cell_after, read(jnp.minimum(i + 1, nx - 1)))
                    else:
                        nxt = read(i + 1)
                    write(i, scratch[i] + (part + NEAR * (nxt - before)))
                low = low + grown[k] * edge
                before, here = here, nxt

                i = highs - k
                part = high if k == 0 else power[k] * high
                edge = after - there
                if first:
                    nxt = read(i - 1)
                    scratch[i] = part
                else:
                    if k == unroll - 1:
                        nxt = jnp.where(b == blocks - 1, cell_before, read(jnp.maximum(i - 1, 0)))
                    else:
                        nxt = read(i - 1)
                    write(i, scratch[i] + (part + NEAR * (after - nxt)))
                high = high + grown[k] * edge
                after, there = there, nxt
            return power[unroll] * low, before, here, power[unroll] * high, after, there

        return step

    carry = (TAIL * sum_before, cell_before, read(0), TAIL * sum_after, cell_after, read(nx - 1))
    carry = lax.fori_loop(0, blocks, sweep(True), carry)
    pieces = 2
    for p in range(pieces):
        lo, hi = p * blocks // pieces, (p + 1) * blocks // pieces
        carry = lax.fori_loop(lo, hi, sweep(False), carry)
        if done is not None:
            done(half + lo * unroll, (hi - lo) * unroll)
            done(half - hi * unroll, (hi - lo) * unroll)


class Outbox:
    def __init__(self, sems):
        self.sems, self.copies = sems, []

    def send(self, src, dst):
        copy = pltpu.make_async_copy(src, dst, self.sems.at[len(self.copies)])
        copy.start()
        self.copies.append(copy)

    def wait(self):
        for copy in self.copies:
            copy.wait()


def params(mib=8):
    return pltpu.CompilerParams(vmem_limit_bytes=mib * 2**20)


def cost(fields, size):
    return pl.CostEstimate(flops=fields * size * 512, transcendentals=0, bytes_accessed=fields * size * 8)


def inner_z(velocity, inner):
    _, nx, ny, nz = velocity.shape
    rows = nx * ny

    def body(v_ref, m_ref, w_out, u_out, v_out, *c_outs):
        outs = (u_out, v_out, w_out) + c_outs
        keep = lax.broadcasted_iota(jnp.int32, (rows, LANES), 1) < LANES - 1
        both = jnp.concatenate([m_ref[0], m_ref[0]], 0)
        w = v_ref[2].reshape(rows, nz)
        for c in range(6):
            f = v_ref[c % 3].reshape(rows, nz)
            if c >= 3:
                f = f * w
            e = jnp.where(keep, pltpu.roll(f, LANES - 1, 1) - f, 0.0)
            hi, lo = split2(e)
            g = dot(jnp.concatenate([hi, lo], 1), both) + dot(hi, m_ref[1])
            outs[c][...] = g.reshape(nx, ny, nz)

    return pl.pallas_call(
        body,
        in_specs=[VMEM, VMEM],
        out_specs=[VMEM] * 6,
        out_shape=[jax.ShapeDtypeStruct(velocity.shape[1:], F32)] * 6,
        compiler_params=params(),
        name="inner_z",
        cost_estimate=cost(6, nx * ny * nz),
    )(velocity, inner)


def slopes_first(velocity, inner, x_halo, z_halo, rims):
    _, nx, ny, nz = velocity.shape
    sub = LANES // ny
    chunks = nx // sub
    rows = nx * ny

    def body(v_ref, i_ref, xl, xr, zl, zr, own_l, own_r, m_ref, gu, gw, sx, sz, st, scratch, rim):
        used = 12 * len(Z_SUMS)
        rim[:, used:, :] = jnp.zeros((chunks, LANES - used, LANES), F32)
        for f in range(6):
            cells = [r[6 + f % 3] for r in (zl, own_l, own_r, zr)]
            if f >= 3:
                cells = [c * r[8] for c, r in zip(cells, (zl, own_l, own_r, zr))]
            terms = [cells[1] - cells[0], zl[f], cells[3] - cells[2], zr[f]]
            for q, term in enumerate(terms):
                hi = term.astype(BF16).astype(F32)
                lo = (term - hi).astype(BF16).astype(F32)
                rim[:, 12 * f + q, :] = hi
                rim[:, 12 * f + 4 + q, :] = lo
                rim[:, 12 * f + 8 + q, :] = hi
        for c in range(chunks):
            st[c * LANES : (c + 1) * LANES] = rim[c].T.astype(BF16)

        g = i_ref[...].reshape(rows, nz) + dot(st[...], m_ref[2])
        gw[...] = g.reshape(nx, ny, nz)

        def write_x(i, g):
            gu[i] = g

        x_derivative(lambda i: v_ref[0, i], write_x, scratch, nx, xl[0], xl[6], xr[0], xr[6])

        zero = jnp.zeros((ny, nz), F32)
        ways = 4

        def add(b, carry):
            out = []
            for k, (total, moment) in enumerate(carry):
                for n in range(2):
                    i = b * 2 * ways + 2 * k + n
                    g = gw[i]
                    total = total + g
                    moment = moment + (i.astype(F32) - 0.5 * (nx - 1)) * g
                out.append((total, moment))
            return tuple(out)

        got = lax.fori_loop(0, nx // (2 * ways), add, ((zero, zero),) * ways)
        sx[0] = (got[0][0] + got[1][0]) + (got[2][0] + got[3][0])
        sx[1] = (got[0][1] + got[1][1]) + (got[2][1] + got[3][1])

        at = lax.broadcasted_iota(jnp.int32, (nz, LANES), 0).astype(F32) - 0.5 * (nz - 1)
        totals, moments = [], []
        for c in range(chunks):
            t = gu[c * sub : (c + 1) * sub].reshape(LANES, nz).T
            totals.append(jnp.sum(t, axis=0, keepdims=True))
            moments.append(jnp.sum(t * at, axis=0, keepdims=True))
        sz[0] = jnp.concatenate(totals, 0)
        sz[1] = jnp.concatenate(moments, 0)

    one = jax.ShapeDtypeStruct(velocity.shape[1:], F32)
    sx = jax.ShapeDtypeStruct((2, ny, nz), F32)
    sz = jax.ShapeDtypeStruct((2, chunks, LANES), F32)
    st = jax.ShapeDtypeStruct((rows, LANES), BF16)
    small = [*x_halo, *z_halo, rims]
    outs = [one, one, sx, sz, st]
    return pl.pallas_call(
        body,
        in_specs=[VMEM] * (2 + len(small)),
        out_specs=[VMEM] * len(outs),
        out_shape=outs,
        scratch_shapes=[pltpu.VMEM((nx, ny, nz), F32), pltpu.VMEM((chunks, LANES, LANES), F32)],
        compiler_params=params(),
        name="slopes_first",
        cost_estimate=cost(2, nx * ny * nz),
    )(velocity, inner, *small)


def slopes_x(velocity, x_halo, gu):
    _, nx, ny, nz = velocity.shape

    def body(v_ref, gu_ref, xl, xr, out, scratch, made, sems):
        box = Outbox(sems)
        box.send(gu_ref, out.at[0])
        for c in (1, 2):

            def write(i, g):
                made[c - 1, i] = g

            def done(start, size):
                rows = pl.ds(start, size)
                box.send(made.at[c - 1, rows], out.at[c, rows])

            x_derivative(
                lambda i: v_ref[c, i], write, scratch, nx, xl[c], xl[6 + c], xr[c], xr[6 + c], done
            )
        box.wait()

    return pl.pallas_call(
        body,
        in_specs=[VMEM] * 4,
        out_specs=ANY,
        out_shape=jax.ShapeDtypeStruct(velocity.shape, F32),
        scratch_shapes=[
            pltpu.VMEM((nx, ny, nz), F32),
            pltpu.VMEM((2, nx, ny, nz), F32),
            pltpu.SemaphoreType.DMA((16,)),
        ],
        compiler_params=params(),
        name="slopes_x",
        cost_estimate=cost(2, nx * ny * nz),
    )(velocity, gu, *x_halo)


def slopes_z(inner_u, inner_v, st, rims, gw):
    nx, ny, nz = gw.shape
    rows = nx * ny
    parts = 2

    def body(iu_ref, iv_ref, gw_ref, st_ref, m_ref, out, made, sems):
        box = Outbox(sems)
        box.send(gw_ref, out.at[2])
        for c, i_ref in enumerate((iu_ref, iv_ref)):
            for p in range(parts):
                at = pl.ds(p * nx // parts, nx // parts)
                local = i_ref[at].reshape(rows // parts, nz)
                g = local + dot(st_ref[pl.ds(p * rows // parts, rows // parts)], m_ref[c])
                made[c, at] = g.reshape(nx // parts, ny, nz)
                box.send(made.at[c, at], out.at[c, at])
        box.wait()

    return pl.pallas_call(
        body,
        in_specs=[VMEM] * 5,
        out_specs=ANY,
        out_shape=jax.ShapeDtypeStruct((3, nx, ny, nz), F32),
        scratch_shapes=[pltpu.VMEM((2, nx, ny, nz), F32), pltpu.SemaphoreType.DMA((16,))],
        compiler_params=params(),
        name="slopes_z",
        cost_estimate=cost(2, nx * ny * nz),
    )(inner_u, inner_v, gw, st, rims)


def divergence(velocity, inner, x_halo, st, rims, comps, into=None):
    _, nx, ny, nz = velocity.shape
    rows = nx * ny

    def body(v_ref, xl, xr, st_ref, m_ref, *rest):
        i_refs = rest[: len(comps)]
        out, scratch, flux, made, sems = rest[-5:]
        box = Outbox(sems)
        for n, c in enumerate(comps):
            flux[...] = v_ref[0] * v_ref[c]
            g = i_refs[n][...].reshape(rows, nz) + dot(st_ref[...], m_ref[3 + c])
            made[n] = g.reshape(nx, ny, nz)

            def write(i, g):
                made[n, i] = made[n, i] + g

            def done(start, size):
                at = pl.ds(start, size)
                box.send(made.at[n, at], out.at[c, at])

            x_derivative(
                lambda i: flux[i],
                write,
                scratch,
                nx,
                xl[3 + c],
                xl[6] * xl[6 + c],
                xr[3 + c],
                xr[6] * xr[6 + c],
                done,
            )
        box.wait()

    extra = [] if into is None else [into]
    return pl.pallas_call(
        body,
        in_specs=[VMEM] * (5 + len(comps)) + [ANY] * len(extra),
        out_specs=ANY,
        out_shape=jax.ShapeDtypeStruct(velocity.shape, F32),
        scratch_shapes=[
            pltpu.VMEM((nx, ny, nz), F32),
            pltpu.VMEM((nx, ny, nz), F32),
            pltpu.VMEM((len(comps), nx, ny, nz), F32),
            pltpu.SemaphoreType.DMA((16,)),
        ],
        input_output_aliases={5 + len(comps): 0} if extra else {},
        compiler_params=params(),
        name="divergence",
        cost_estimate=cost(2 * len(comps), nx * ny * nz),
    )(velocity, *x_halo, st, rims, *inner, *extra)


def rebuild(gu, gw, x_terms, z_terms, mats, total_x, total_z):
    nx, ny, nz = gu.shape
    sub = LANES // ny
    chunks = nx // sub
    rows = nx * ny
    parts = 4
    scale_x = -1.0 / math.sqrt(total_x)
    scale_z = -1.0 / math.sqrt(total_z)

    def body(u_ref, w_ref, xt, zt, m_ref, out, rim, made, sems):
        box = Outbox(sems)
        rim[:, 6:, :] = jnp.zeros((chunks, LANES - 6, LANES), F32)
        for q in range(2):
            for p, part in enumerate(split3(zt[q])):
                rim[:, 3 * q + p, :] = part.astype(F32)
        for p in range(parts):
            at = pl.ds(p * nx // parts, nx // parts)
            hi, mid, lo = split3(u_ref[at].reshape(rows // parts, nz))
            here = range(p * chunks // parts, (p + 1) * chunks // parts)
            st = jnp.concatenate([rim[c].T.astype(BF16) for c in here], 0)
            g = dot(jnp.concatenate([hi, mid], 1), m_ref[0]) + dot(
                jnp.concatenate([lo, st], 1), m_ref[1]
            )
            made[1, at] = (scale_z * g).reshape(nx // parts, ny, nz)
            box.send(made.at[1, at], out.at[1, at])

        mean = xt[1]

        def along_x(b, acc):
            for k in range(8):
                i = b * 8 + k
                g = w_ref[i]
                made[0, i] = scale_x * (acc + 0.5 * g)
                acc = acc + (g - mean)
            return acc

        acc = xt[0]
        for p in range(parts):
            acc = lax.fori_loop(p * nx // parts // 8, (p + 1) * nx // parts // 8, along_x, acc)
            at = pl.ds(p * nx // parts, nx // parts)
            box.send(made.at[0, at], out.at[0, at])
        box.wait()

    shape = (2,) + gu.shape
    return pl.pallas_call(
        body,
        in_specs=[VMEM] * 5,
        out_specs=ANY,
        out_shape=jax.ShapeDtypeStruct(shape, F32),
        scratch_shapes=[
            pltpu.VMEM((chunks, LANES, LANES), F32),
            pltpu.VMEM(shape, F32),
            pltpu.SemaphoreType.DMA((16,)),
        ],
        compiler_params=params(),
        name="rebuild",
        cost_estimate=cost(2, nx * ny * nz),
    )(gu, gw, x_terms, z_terms, mats)


def swap(axis, up, down):
    n = lax.axis_size(axis)
    before = lax.ppermute(up, axis, [(i, (i + 1) % n) for i in range(n)])
    after = lax.ppermute(down, axis, [((i + 1) % n, i) for i in range(n)])
    return before, after


def exchange(axis, terms, bit):
    n = lax.axis_size(axis)
    return lax.ppermute(terms, axis, [(i, i ^ bit) for i in range(n)])


def combine(terms, before, part, upper):
    return terms + part, before + upper * part[0]


def place(axis, cells):
    n = lax.axis_size(axis)
    mine = lax.axis_index(axis)
    bits = {}
    bit = 1
    while bit < n:
        bits[bit] = jnp.where((mine & bit) != 0, 1.0, 0.0).astype(F32)
        bit *= 2
    start = (mine * cells).astype(F32)
    centre = start + (0.5 * (cells - 1) - 0.5 * (n * cells - 1))
    return bits, centre, (start + 0.5) * (1.0 / (n * cells))


def line_terms(terms, before, start, total_len):
    mean = terms[0] / total_len
    offset = before - start * terms[0] + terms[1] / total_len
    return jnp.stack([offset, mean])


def body(velocity):
    _, nx, ny, nz = velocity.shape
    size_x = lax.axis_size("gx")
    size_z = lax.axis_size("gz")
    total_x = nx * size_x
    total_z = nz * size_z
    inner_mats = jnp.asarray(z_inner())
    rims = jnp.asarray(z_rims(len(Z_SUMS)))
    sums = jnp.asarray(sum_matrices())

    spot_x, spot_z = place("gx", nx), place("gz", nz)
    velocity, (spot_x, spot_z) = lax.optimization_barrier((velocity, (spot_x, spot_z)))
    bits_x, centre_x, x0 = spot_x
    bits_z, centre_z, z0 = spot_z
    xu, xd, zu, zd, vel = edges_call(velocity)
    z_halo = (*swap("gz", zu, zd), zd, zu)
    x_halo = swap("gx", xu, xd)
    in_w, in_u, in_v, *in_c = inner_z(vel, inner_mats)
    gu, gw, sx, sz, st = slopes_first(vel, in_w, x_halo, z_halo, rims)

    tx = jnp.stack([sx[0], sx[1] + centre_x * sx[0]])
    tz = jnp.stack([sz[0], sz[1] + centre_z * sz[0]])
    bx = jnp.zeros_like(sx[0])
    bz = jnp.zeros_like(sz[0])

    results = {}
    fillers = [
        ("gx", lambda: slopes_x(vel, x_halo, gu)),
        ("gz", lambda: slopes_z(in_u, in_v, st, rims, gw)),
        ("c0", lambda: divergence(vel, in_c[:1], x_halo, st, rims, [0])),
        ("c1", lambda: divergence(vel, in_c[1:], x_halo, st, rims, [1, 2], results["c0"])),
    ]
    bit = 1
    while bit < max(size_x, size_z) or fillers:
        px = exchange("gx", tx, bit) if bit < size_x else None
        pz = exchange("gz", tz, bit) if bit < size_z else None
        if fillers:
            name, make = fillers.pop(0)
            results[name] = make()
            px, pz, results[name] = lax.optimization_barrier((px, pz, results[name]))
        if px is not None:
            tx, bx = combine(tx, bx, px, bits_x[bit])
        if pz is not None:
            tz, bz = combine(tz, bz, pz, bits_z[bit])
        bit *= 2
    rebuilt = rebuild(
        gu,
        gw,
        line_terms(tx, bx, x0, total_x),
        line_terms(tz, bz, z0, total_z),
        sums,
        total_x,
        total_z,
    )
    return (results["gx"], results["gz"], results["c1"], rebuilt)


def solution(mesh):
    spec = P(None, "gx", None, "gz")
    return jax.shard_map(
        body, mesh=mesh, in_specs=(spec,), out_specs=(spec,) * 4, check_vma=False
    )
```

```python
import math

import jax
import jax.numpy as jnp
import numpy as np
from jax import lax
from jax.experimental import pallas as pl
from jax.experimental.pallas import tpu as pltpu
from jax.sharding import PartitionSpec as P

ALPHA = 1.0 / 3.0
COEF_A = 14.0 / 9.0
COEF_B = 1.0 / 9.0
LANES = 128
F32 = jnp.float32
VMEM = pl.BlockSpec(memory_space=pltpu.VMEM)
HBM = pl.BlockSpec(memory_space=pltpu.HBM)
ANY = pl.BlockSpec(memory_space=pl.ANY)
BF16 = jnp.bfloat16

RHO = (-1.0 + math.sqrt(1.0 - 4.0 * ALPHA * ALPHA)) / (2.0 * ALPHA)


def kernel_weights():
    reach = 400
    k = np.arange(-reach, reach + 1)
    green = RHO ** np.abs(k).astype(np.float64) / math.sqrt(1.0 - 4.0 * ALPHA * ALPHA)

    def shifted(s):
        out = np.zeros_like(green)
        if s >= 0:
            out[s:] = green[: len(green) - s]
        else:
            out[:s] = green[-s:]
        return out

    direct = 0.5 * COEF_A * (shifted(-1) - shifted(1)) + 0.25 * COEF_B * (shifted(-2) - shifted(2))
    total = np.concatenate([[0.0], np.cumsum(direct)])
    return {m: total[m + reach] for m in range(-2, 4)}


_W = kernel_weights()
NEAR = _W[1]
TAIL = _W[2] / RHO**2
KAPPA = TAIL * RHO * RHO
TOGETHER = 16
REACH = 96


def h_of(m):
    m = np.asarray(m)
    m = np.where(m <= 0, 1 - m, m)
    return np.where(m == 1, NEAR, TAIL * RHO ** m.astype(np.float64))


def split_np(x):
    hi = x.astype(BF16)
    lo = (x - hi.astype(np.float64)).astype(BF16)
    return hi, lo


def going_up(length):
    j = np.arange(length)
    w = (RHO - 1.0) * RHO ** (length - j).astype(np.float64)
    w[-1] = RHO**2
    return w


def going_down(length):
    return going_up(length)[::-1] * -1.0


def z_inner():
    j = np.arange(LANES)
    inner = h_of(j[None, :] - j[:, None])
    inner[LANES - 1] = 0.0
    hi, lo = split_np(inner)
    return np.stack([hi, lo])


def z_rims(fields):
    j = np.arange(LANES)
    rim = np.stack(
        [
            h_of(j + 1),
            TAIL * RHO ** j.astype(np.float64),
            h_of(LANES - j),
            TAIL * RHO ** (LANES - 1 - j).astype(np.float64),
        ]
    )
    hi, lo = split_np(rim)
    out = np.zeros((fields, LANES, LANES), BF16)
    for f in range(fields):
        out[f, 12 * f : 12 * f + 12] = np.concatenate([hi, hi, lo], 0)
    return out


def sum_matrices():
    j = np.arange(LANES)
    lower = (j[:, None] < j[None, :]) + 0.5 * (j[:, None] == j[None, :])
    ones = np.ones((3, LANES))
    slope = -np.broadcast_to(j, (3, LANES))
    pad = np.zeros((LANES - 6, LANES))
    first = np.concatenate([lower, lower], 0)
    second = np.concatenate([lower, ones, slope, pad], 0)
    return np.stack([first, second]).astype(BF16)


def split2(x):
    hi = x.astype(BF16)
    return hi, (x - hi.astype(F32)).astype(BF16)


def split3(x):
    hi = x.astype(BF16)
    rest = x - hi.astype(F32)
    mid = rest.astype(BF16)
    return hi, mid, (rest - mid.astype(F32)).astype(BF16)


def dot(a, b):
    return lax.dot_general(a, b, (((1,), (0,)), ((), ())), preferred_element_type=F32)


def product(values, name):
    out = values[name[0]]
    for c in name[1:]:
        out = out * values[c]
    return out


COMP = {"u": 0, "v": 1, "w": 2}


X_SUMS = ["u", "v", "w", "uu", "uv", "uw"]
Z_SUMS = ["u", "v", "w", "wu", "wv", "ww"]
CELLS = ["u", "v", "w"]


def z_weights(nz, cut):
    row = lax.broadcasted_iota(jnp.int32, (8, LANES), 0)

    def tiles(powers, factors):
        tile = jnp.zeros((8, LANES), F32)
        for k in range(8):
            tile = jnp.where(row == k, np.float32(powers[k]), tile)
        return [tile * np.float32(f) for f in factors]

    up = going_up(nz)[nz - cut :]
    down = going_down(nz)[:cut]
    ups = tiles(up[:8] / up[0], up[::8])
    ups[-1] = jnp.where(row == 7, np.float32(up[-1]), ups[-1])
    steady = down[8:16] / down[8]
    downs = tiles(steady, [down[8] / RHO**8] + list(down[8::8]))
    downs[0] = jnp.where(row == 0, np.float32(down[0]), downs[0])
    return jnp.concatenate(ups, 0), jnp.concatenate(downs, 0)


def edges_call(velocity):
    _, nx, ny, nz = velocity.shape
    sub = LANES // ny
    chunks = nx // sub
    nq = len(Z_SUMS) + len(CELLS)
    cut_x = min(REACH, nx)
    cut = min(REACH, nz)
    group = 8
    parts = 8
    part = nx // parts

    def body(v_hbm, xu_ref, xd_ref, zu_ref, zd_ref, v_ref, sems):
        copies = [
            pltpu.make_async_copy(
                v_hbm.at[:, pl.ds(p * part, part)], v_ref.at[:, pl.ds(p * part, part)], sems.at[p]
            )
            for p in range(parts)
        ]
        for copy in copies:
            copy.start()
        weight_up, weight_down = z_weights(nz, cut)

        def x_rows(acc, weights, rows):
            for i in rows:
                vals = {c: v_ref[COMP[c], i] for c in CELLS}
                for q, name in enumerate(X_SUMS):
                    term = product(vals, name) * np.float32(weights[i])
                    acc[q] = term if acc[q] is None else acc[q] + term

        ups = [None] * len(X_SUMS)
        downs = [None] * len(X_SUMS)
        rows = {}
        for p in range(parts):
            copies[p].wait()
            for s in range(p * part // sub, (p + 1) * part // sub):
                t = {c: v_ref[COMP[c], s * sub : (s + 1) * sub].reshape(LANES, nz).T for c in CELLS}
                for q, name in enumerate(Z_SUMS):
                    f = product(t, name)
                    up = jnp.sum(f[nz - cut :] * weight_up, axis=0, keepdims=True)
                    down = jnp.sum(f[:cut] * weight_down, axis=0, keepdims=True)
                    rows.setdefault(q, []).append((up, down))
                for q, name in enumerate(CELLS):
                    rows.setdefault(len(Z_SUMS) + q, []).append((t[name][nz - 1 : nz], t[name][0:1]))
                if (s + 1) % group == 0:
                    at = s + 1 - group
                    for q, pairs in rows.items():
                        zu_ref[q, at : at + group] = jnp.concatenate([r[0] for r in pairs], 0)
                        zd_ref[q, at : at + group] = jnp.concatenate([r[1] for r in pairs], 0)
                    rows = {}
            here = range(p * part, (p + 1) * part)
            x_rows(downs, going_down(nx), [i for i in here if i < cut_x])
            x_rows(ups, going_up(nx), [i for i in here if i >= nx - cut_x])
        for q in range(len(X_SUMS)):
            xu_ref[q] = ups[q]
            xd_ref[q] = downs[q]
        for q in range(len(CELLS)):
            xu_ref[len(X_SUMS) + q] = v_ref[q, nx - 1]
            xd_ref[len(X_SUMS) + q] = v_ref[q, 0]

    xs = jax.ShapeDtypeStruct((nq, ny, nz), F32)
    zs = jax.ShapeDtypeStruct((nq, chunks, LANES), F32)
    return pl.pallas_call(
        body,
        in_specs=[HBM],
        out_specs=[VMEM] * 5,
        out_shape=[xs, xs, zs, zs, jax.ShapeDtypeStruct(velocity.shape, F32)],
        scratch_shapes=[pltpu.SemaphoreType.DMA((parts,))],
        compiler_params=params(),
        name="edges",
        cost_estimate=cost(6, nx * ny * nz),
    )(pltpu.with_memory_space_constraint(velocity, pltpu.HBM))


def x_derivatives(read, write, scratch, nx, rims, pieces=1, done=None):
    unroll = 8
    half = nx // 2
    blocks = half // unroll
    fields = range(len(rims))
    grown = [KAPPA * RHO ** -(k + 1) for k in range(unroll)]
    power = [RHO**k for k in range(unroll + 1)]

    def sweep(first):
        def step(b, carry):
            out = []
            lows = (0 if first else half) + b * unroll
            highs = (nx if first else half) - 1 - b * unroll
            for f in fields:
                low, before, here, high, after, there = carry[f]
                _, cell_before, _, cell_after = rims[f]
                for k in range(unroll):
                    i = lows + k
                    part = low if k == 0 else power[k] * low
                    edge = here - before
                    if first:
                        nxt = read(f, i + 1)
                        scratch(f)[i] = part
                    else:
                        if k == unroll - 1:
                            inside = read(f, jnp.minimum(i + 1, nx - 1))
                            nxt = jnp.where(b == blocks - 1, cell_after, inside)
                        else:
                            nxt = read(f, i + 1)
                        write(f, i, scratch(f)[i] + (part + NEAR * (nxt - before)))
                    low = low + grown[k] * edge
                    before, here = here, nxt

                    i = highs - k
                    part = high if k == 0 else power[k] * high
                    edge = after - there
                    if first:
                        nxt = read(f, i - 1)
                        scratch(f)[i] = part
                    else:
                        if k == unroll - 1:
                            inside = read(f, jnp.maximum(i - 1, 0))
                            nxt = jnp.where(b == blocks - 1, cell_before, inside)
                        else:
                            nxt = read(f, i - 1)
                        write(f, i, scratch(f)[i] + (part + NEAR * (after - nxt)))
                    high = high + grown[k] * edge
                    after, there = there, nxt
                out.append((power[unroll] * low, before, here, power[unroll] * high, after, there))
            return tuple(out)

        return step

    carry = tuple(
        (TAIL * sum_before, cell_before, read(f, 0), TAIL * sum_after, cell_after, read(f, nx - 1))
        for f, (sum_before, cell_before, sum_after, cell_after) in enumerate(rims)
    )
    carry = lax.fori_loop(0, blocks, sweep(True), carry)
    for p in range(pieces):
        lo, hi = p * blocks // pieces, (p + 1) * blocks // pieces
        carry = lax.fori_loop(lo, hi, sweep(False), carry)
        if done is not None:
            done(half + lo * unroll, (hi - lo) * unroll)
            done(half - hi * unroll, (hi - lo) * unroll)


class Outbox:
    def __init__(self, sems):
        self.sems, self.copies = sems, []

    def send(self, src, dst):
        copy = pltpu.make_async_copy(src, dst, self.sems.at[len(self.copies)])
        copy.start()
        self.copies.append(copy)

    def wait(self):
        for copy in self.copies:
            copy.wait()


def params(mib=8):
    return pltpu.CompilerParams(vmem_limit_bytes=mib * 2**20)


def cost(fields, size):
    return pl.CostEstimate(flops=fields * size * 512, transcendentals=0, bytes_accessed=fields * size * 8)


def inner_z(velocity, inner):
    _, nx, ny, nz = velocity.shape
    rows = nx * ny

    def body(v_ref, m_ref, w_out, u_out, v_out, *c_outs):
        outs = (u_out, v_out, w_out) + c_outs
        keep = lax.broadcasted_iota(jnp.int32, (rows, LANES), 1) < LANES - 1
        both = jnp.concatenate([m_ref[0], m_ref[0]], 0)
        w = v_ref[2].reshape(rows, nz)
        for c in range(6):
            f = v_ref[c % 3].reshape(rows, nz)
            if c >= 3:
                f = f * w
            e = jnp.where(keep, pltpu.roll(f, LANES - 1, 1) - f, 0.0)
            hi, lo = split2(e)
            g = dot(jnp.concatenate([hi, lo], 1), both) + dot(hi, m_ref[1])
            outs[c][...] = g.reshape(nx, ny, nz)

    return pl.pallas_call(
        body,
        in_specs=[VMEM, VMEM],
        out_specs=[VMEM] * 6,
        out_shape=[jax.ShapeDtypeStruct(velocity.shape[1:], F32)] * 6,
        compiler_params=params(),
        name="inner_z",
        cost_estimate=cost(6, nx * ny * nz),
    )(velocity, inner)


def slopes_first(velocity, inner, x_halo, z_halo, rims):
    _, nx, ny, nz = velocity.shape
    sub = LANES // ny
    chunks = nx // sub
    rows = nx * ny

    def body(v_ref, i_ref, xl, xr, zl, zr, own_l, own_r, m_ref, gu, gw, tx, tz, st, px, pz, scratch, rim):
        used = 12 * len(Z_SUMS)
        rim[:, used:, :] = jnp.zeros((chunks, LANES - used, LANES), F32)
        for f in range(6):
            cells = [r[6 + f % 3] for r in (zl, own_l, own_r, zr)]
            if f >= 3:
                cells = [c * r[8] for c, r in zip(cells, (zl, own_l, own_r, zr))]
            terms = [cells[1] - cells[0], zl[f], cells[3] - cells[2], zr[f]]
            for q, term in enumerate(terms):
                hi = term.astype(BF16).astype(F32)
                lo = (term - hi).astype(BF16).astype(F32)
                rim[:, 12 * f + q, :] = hi
                rim[:, 12 * f + 4 + q, :] = lo
                rim[:, 12 * f + 8 + q, :] = hi
        for c in range(chunks):
            st[c * LANES : (c + 1) * LANES] = rim[c].T.astype(BF16)

        g = i_ref[...].reshape(rows, nz) + dot(st[...], m_ref[2])
        gw[...] = g.reshape(nx, ny, nz)

        def write_x(_, i, g):
            gu[i] = g

        rims_x = [(xl[0], xl[6], xr[0], xr[6])]
        x_derivatives(lambda _, i: v_ref[0, i], write_x, lambda _: scratch, nx, rims_x)

        zero = jnp.zeros((ny, nz), F32)
        ways = 4

        def add(b, carry):
            out = []
            for k, (total, moment) in enumerate(carry):
                for n in range(2):
                    i = b * 2 * ways + 2 * k + n
                    g = gw[i]
                    total = total + g
                    moment = moment + (i.astype(F32) - 0.5 * (nx - 1)) * g
                out.append((total, moment))
            return tuple(out)

        got = lax.fori_loop(0, nx // (2 * ways), add, ((zero, zero),) * ways)
        bits, centre, start = place("gx", nx)
        total = (got[0][0] + got[1][0]) + (got[2][0] + got[3][0])
        tx[0] = total
        tx[1] = (got[0][1] + got[1][1]) + (got[2][1] + got[3][1]) + centre * total
        for k, value in enumerate([*bits, start]):
            px[k] = jnp.full((ny, nz), value, F32)

        at = lax.broadcasted_iota(jnp.int32, (nz, LANES), 0).astype(F32) - 0.5 * (nz - 1)
        totals, moments = [], []
        for c in range(chunks):
            t = gu[c * sub : (c + 1) * sub].reshape(LANES, nz).T
            totals.append(jnp.sum(t, axis=0, keepdims=True))
            moments.append(jnp.sum(t * at, axis=0, keepdims=True))
        bits, centre, start = place("gz", nz)
        total = jnp.concatenate(totals, 0)
        tz[0] = total
        tz[1] = jnp.concatenate(moments, 0) + centre * total
        for k, value in enumerate([*bits, start]):
            pz[k] = jnp.full((chunks, LANES), value, F32)

    one = jax.ShapeDtypeStruct(velocity.shape[1:], F32)
    sx = jax.ShapeDtypeStruct((2, ny, nz), F32)
    sz = jax.ShapeDtypeStruct((2, chunks, LANES), F32)
    st = jax.ShapeDtypeStruct((rows, LANES), BF16)
    small = [*x_halo, *z_halo, rims]
    steps_x = sum(count - 1 for count, _ in LEVELS["gx"])
    steps_z = sum(count - 1 for count, _ in LEVELS["gz"])
    px = jax.ShapeDtypeStruct((steps_x + 1, ny, nz), F32)
    pz = jax.ShapeDtypeStruct((steps_z + 1, chunks, LANES), F32)
    outs = [one, one, sx, sz, st, px, pz]
    return pl.pallas_call(
        body,
        in_specs=[VMEM] * (2 + len(small)),
        out_specs=[VMEM] * len(outs),
        out_shape=outs,
        scratch_shapes=[pltpu.VMEM((nx, ny, nz), F32), pltpu.VMEM((chunks, LANES, LANES), F32)],
        compiler_params=params(),
        name="slopes_first",
        cost_estimate=cost(2, nx * ny * nz),
    )(velocity, inner, *small)


def slopes_rest(velocity, inner_u, inner_v, x_halo, st, rims, gw):
    _, nx, ny, nz = velocity.shape
    rows = nx * ny
    parts = 2

    def body(v_ref, iu_ref, iv_ref, xl, xr, st_ref, m_ref, gw_ref, gv, gx, out, s0, s1, made, sems):
        box = Outbox(sems)
        box.send(gw_ref, out.at[2])
        for c, i_ref in enumerate((iu_ref, iv_ref)):
            for p in range(parts):
                at = pl.ds(p * nx // parts, nx // parts)
                local = i_ref[at].reshape(rows // parts, nz)
                g = local + dot(st_ref[pl.ds(p * rows // parts, rows // parts)], m_ref[c])
                made[c, at] = g.reshape(nx // parts, ny, nz)
                box.send(made.at[c, at], out.at[c, at])

        def write(f, i, g):
            (gv, gx)[f][i] = g

        x_derivatives(
            lambda f, i: v_ref[1 + f, i],
            write,
            lambda f: (s0, s1)[f],
            nx,
            [(xl[c], xl[6 + c], xr[c], xr[6 + c]) for c in (1, 2)],
        )
        box.wait()

    one = jax.ShapeDtypeStruct((nx, ny, nz), F32)
    return pl.pallas_call(
        body,
        in_specs=[VMEM] * 8,
        out_specs=[VMEM, VMEM, ANY],
        out_shape=[one, one, jax.ShapeDtypeStruct(velocity.shape, F32)],
        scratch_shapes=[
            pltpu.VMEM((nx, ny, nz), F32),
            pltpu.VMEM((nx, ny, nz), F32),
            pltpu.VMEM((2, nx, ny, nz), F32),
            pltpu.SemaphoreType.DMA((8,)),
        ],
        compiler_params=params(),
        name="slopes_rest",
        cost_estimate=cost(3, nx * ny * nz),
    )(velocity, inner_u, inner_v, *x_halo, st, rims, gw)


def divergence(velocity, inner, x_halo, st, rims, slopes):
    _, nx, ny, nz = velocity.shape
    rows = nx * ny
    comps = range(3)

    def body(v_ref, xl, xr, st_ref, m_ref, *rest):
        i_refs, g_refs = rest[:3], rest[3:6]
        gx, out, s0, s1, s2, m0, m1, m2, sems = rest[6:]
        made = (m0, m1, m2)
        box = Outbox(sems)
        for c in comps:
            box.send(g_refs[c], gx.at[c])
        for c in comps:
            g = i_refs[c][...].reshape(rows, nz) + dot(st_ref[...], m_ref[3 + c])
            made[c][...] = g.reshape(nx, ny, nz)

        def write(c, i, g):
            made[c][i] = made[c][i] + g

        def done(start, size):
            at = pl.ds(start, size)
            for c in comps:
                box.send(made[c].at[at], out.at[c, at])

        x_derivatives(
            lambda c, i: v_ref[0, i] * v_ref[c, i],
            write,
            lambda c: (s0, s1, s2)[c],
            nx,
            [(xl[3 + c], xl[6] * xl[6 + c], xr[3 + c], xr[6] * xr[6 + c]) for c in comps],
            4,
            done,
        )
        box.wait()

    full = jax.ShapeDtypeStruct(velocity.shape, F32)
    return pl.pallas_call(
        body,
        in_specs=[VMEM] * 11,
        out_specs=[ANY, ANY],
        out_shape=[full, full],
        scratch_shapes=[pltpu.VMEM((nx, ny, nz), F32)] * 6 + [pltpu.SemaphoreType.DMA((32,))],
        compiler_params=params(12),
        name="divergence",
        cost_estimate=cost(6, nx * ny * nz),
    )(velocity, *x_halo, st, rims, *inner, *slopes)


def rebuild(gu, gw, x_terms, z_terms, mats, total_x, total_z):
    nx, ny, nz = gu.shape
    sub = LANES // ny
    chunks = nx // sub
    rows = nx * ny
    parts = 4
    scale_x = -1.0 / math.sqrt(total_x)
    scale_z = -1.0 / math.sqrt(total_z)

    def body(u_ref, w_ref, xt, zt, m_ref, out, rim, made, sems):
        box = Outbox(sems)
        mean = xt[1]

        def along_x(b, acc):
            for k in range(8):
                i = b * 8 + k
                g = w_ref[i]
                made[0, i] = scale_x * (acc + 0.5 * g)
                acc = acc + (g - mean)
            return acc

        acc = xt[0]
        for p in range(parts):
            acc = lax.fori_loop(p * nx // parts // 8, (p + 1) * nx // parts // 8, along_x, acc)
            at = pl.ds(p * nx // parts, nx // parts)
            box.send(made.at[0, at], out.at[0, at])
        rim[:, 6:, :] = jnp.zeros((chunks, LANES - 6, LANES), F32)
        for q in range(2):
            for p, part in enumerate(split3(zt[q])):
                rim[:, 3 * q + p, :] = part.astype(F32)
        for p in range(parts):
            at = pl.ds(p * nx // parts, nx // parts)
            hi, mid, lo = split3(u_ref[at].reshape(rows // parts, nz))
            here = range(p * chunks // parts, (p + 1) * chunks // parts)
            st = jnp.concatenate([rim[c].T.astype(BF16) for c in here], 0)
            g = dot(jnp.concatenate([hi, mid], 1), m_ref[0]) + dot(
                jnp.concatenate([lo, st], 1), m_ref[1]
            )
            made[1, at] = (scale_z * g).reshape(nx // parts, ny, nz)
            box.send(made.at[1, at], out.at[1, at])
        box.wait()

    shape = (2,) + gu.shape
    return pl.pallas_call(
        body,
        in_specs=[VMEM] * 5,
        out_specs=ANY,
        out_shape=jax.ShapeDtypeStruct(shape, F32),
        scratch_shapes=[
            pltpu.VMEM((chunks, LANES, LANES), F32),
            pltpu.VMEM(shape, F32),
            pltpu.SemaphoreType.DMA((16,)),
        ],
        compiler_params=params(),
        name="rebuild",
        cost_estimate=cost(2, nx * ny * nz),
    )(gu, gw, x_terms, z_terms, mats)


def swap(axis, up, down):
    n = lax.axis_size(axis)
    before = lax.ppermute(up, axis, [(i, (i + 1) % n) for i in range(n)])
    after = lax.ppermute(down, axis, [((i + 1) % n, i) for i in range(n)])
    return before, after


LEVELS = {"gx": [(2, 1), (4, 2)], "gz": [(4, 1), (4, 4)]}


def exchange(axis, terms, level):
    n = lax.axis_size(axis)
    count, stride = level
    parts = {}
    for k in sorted(range(1, count), key=lambda k: min(k, count - k)):
        pairs = []
        for i in range(n):
            own = (i // stride) % count
            pairs.append((i, i + ((own + k) % count - own) * stride))
        parts[k] = lax.ppermute(terms, axis, pairs)
    return parts


def combine(terms, before, parts, lower):
    for k, part in parts.items():
        before = before + lower[k] * part[0]
        terms = terms + part
    return terms, before


def place(axis, cells):
    n = lax.axis_size(axis)
    mine = lax.axis_index(axis)
    below = []
    for count, stride in LEVELS[axis]:
        own = mine // stride % count
        for k in range(1, count):
            below.append((own >= k).astype(F32))
    start = (mine * cells).astype(F32)
    centre = start + (0.5 * (cells - 1) - 0.5 * (n * cells - 1))
    return below, centre, (start + 0.5) * (1.0 / (n * cells))


def below_of(axis, spot, at):
    skip = sum(count - 1 for count, _ in LEVELS[axis][:at])
    count = LEVELS[axis][at][0]
    return {k: spot[skip + k - 1] for k in range(1, count)}


def line_terms(terms, before, start, total_len):
    mean = terms[0] / total_len
    offset = before - start * terms[0] + terms[1] / total_len
    return jnp.stack([offset, mean])


def body(velocity):
    _, nx, ny, nz = velocity.shape
    size_x = lax.axis_size("gx")
    size_z = lax.axis_size("gz")
    total_x = nx * size_x
    total_z = nz * size_z
    inner_mats = jnp.asarray(z_inner())
    rims = jnp.asarray(z_rims(len(Z_SUMS)))
    sums = jnp.asarray(sum_matrices())

    xu, xd, zu, zd, vel = edges_call(velocity)
    z_halo = (*swap("gz", zu, zd), zd, zu)
    x_halo = swap("gx", xu, xd)
    in_w, in_u, in_v, *in_c = inner_z(vel, inner_mats)
    gu, gw, tx, tz, st, spot_x, spot_z = slopes_first(vel, in_w, x_halo, z_halo, rims)
    bx = jnp.zeros_like(tx[0])
    bz = jnp.zeros_like(tz[0])

    px = exchange("gx", tx, LEVELS["gx"][0])
    pz = exchange("gz", tz, LEVELS["gz"][0])
    gv, gq, grad_z = slopes_rest(vel, in_u, in_v, x_halo, st, rims, gw)
    px, pz, gv, gq, grad_z = lax.optimization_barrier((px, pz, gv, gq, grad_z))
    tx, bx = combine(tx, bx, px, below_of("gx", spot_x, 0))
    tz, bz = combine(tz, bz, pz, below_of("gz", spot_z, 0))
    px = exchange("gx", tx, LEVELS["gx"][1])
    pz = exchange("gz", tz, LEVELS["gz"][1])
    grad_x, convect = divergence(vel, in_c, x_halo, st, rims, (gu, gv, gq))
    px, pz, grad_x, convect = lax.optimization_barrier((px, pz, grad_x, convect))
    tx, bx = combine(tx, bx, px, below_of("gx", spot_x, 1))
    tz, bz = combine(tz, bz, pz, below_of("gz", spot_z, 1))
    rebuilt = rebuild(
        gu,
        gw,
        line_terms(tx, bx, spot_x[-1], total_x),
        line_terms(tz, bz, spot_z[-1], total_z),
        sums,
        total_x,
        total_z,
    )
    return (grad_x, grad_z, convect, rebuilt)


def solution(mesh):
    spec = P(None, "gx", None, "gz")
    return jax.shard_map(
        body, mesh=mesh, in_specs=(spec,), out_specs=(spec,) * 4, check_vma=False
    )
```

```python
import math

import jax
import jax.numpy as jnp
import numpy as np
from jax import lax
from jax.experimental import pallas as pl
from jax.experimental.pallas import tpu as pltpu
from jax.sharding import PartitionSpec as P

ALPHA = 1.0 / 3.0
COEF_A = 14.0 / 9.0
COEF_B = 1.0 / 9.0
LANES = 128
F32 = jnp.float32
VMEM = pl.BlockSpec(memory_space=pltpu.VMEM)
HBM = pl.BlockSpec(memory_space=pltpu.HBM)
ANY = pl.BlockSpec(memory_space=pl.ANY)
BF16 = jnp.bfloat16

RHO = (-1.0 + math.sqrt(1.0 - 4.0 * ALPHA * ALPHA)) / (2.0 * ALPHA)


def kernel_weights():
    reach = 400
    k = np.arange(-reach, reach + 1)
    green = RHO ** np.abs(k).astype(np.float64) / math.sqrt(1.0 - 4.0 * ALPHA * ALPHA)

    def shifted(s):
        out = np.zeros_like(green)
        if s >= 0:
            out[s:] = green[: len(green) - s]
        else:
            out[:s] = green[-s:]
        return out

    direct = 0.5 * COEF_A * (shifted(-1) - shifted(1)) + 0.25 * COEF_B * (shifted(-2) - shifted(2))
    total = np.concatenate([[0.0], np.cumsum(direct)])
    return {m: total[m + reach] for m in range(-2, 4)}


_W = kernel_weights()
NEAR = _W[1]
TAIL = _W[2] / RHO**2
KAPPA = TAIL * RHO * RHO
TOGETHER = 16
REACH = 96


def h_of(m):
    m = np.asarray(m)
    m = np.where(m <= 0, 1 - m, m)
    return np.where(m == 1, NEAR, TAIL * RHO ** m.astype(np.float64))


def split_np(x):
    hi = x.astype(BF16)
    lo = (x - hi.astype(np.float64)).astype(BF16)
    return hi, lo


def going_up(length):
    j = np.arange(length)
    w = (RHO - 1.0) * RHO ** (length - j).astype(np.float64)
    w[-1] = RHO**2
    return w


def going_down(length):
    return going_up(length)[::-1] * -1.0


def z_inner():
    j = np.arange(LANES)
    inner = h_of(j[None, :] - j[:, None])
    inner[LANES - 1] = 0.0
    hi, lo = split_np(inner)
    return np.stack([hi, lo])


def z_rims(fields):
    j = np.arange(LANES)
    rim = np.stack(
        [
            h_of(j + 1),
            TAIL * RHO ** j.astype(np.float64),
            h_of(LANES - j),
            TAIL * RHO ** (LANES - 1 - j).astype(np.float64),
        ]
    )
    hi, lo = split_np(rim)
    out = np.zeros((fields, LANES, LANES), BF16)
    for f in range(fields):
        out[f, 12 * f : 12 * f + 12] = np.concatenate([hi, hi, lo], 0)
    return out


def sum_matrices():
    j = np.arange(LANES)
    lower = (j[:, None] < j[None, :]) + 0.5 * (j[:, None] == j[None, :])
    ones = np.ones((3, LANES))
    slope = -np.broadcast_to(j, (3, LANES))
    pad = np.zeros((LANES - 6, LANES))
    first = np.concatenate([lower, lower], 0)
    second = np.concatenate([lower, ones, slope, pad], 0)
    return np.stack([first, second]).astype(BF16)


def split2(x):
    hi = x.astype(BF16)
    return hi, (x - hi.astype(F32)).astype(BF16)


def split3(x):
    hi = x.astype(BF16)
    rest = x - hi.astype(F32)
    mid = rest.astype(BF16)
    return hi, mid, (rest - mid.astype(F32)).astype(BF16)


def dot(a, b):
    return lax.dot_general(a, b, (((1,), (0,)), ((), ())), preferred_element_type=F32)


def product(values, name):
    out = values[name[0]]
    for c in name[1:]:
        out = out * values[c]
    return out


COMP = {"u": 0, "v": 1, "w": 2}


X_SUMS = ["u", "v", "w", "uu", "uv", "uw"]
Z_SUMS = ["u", "v", "w", "wu", "wv", "ww"]
CELLS = ["u", "v", "w"]


def z_weights(nz, cut):
    row = lax.broadcasted_iota(jnp.int32, (8, LANES), 0)

    def tiles(powers, factors):
        tile = jnp.zeros((8, LANES), F32)
        for k in range(8):
            tile = jnp.where(row == k, np.float32(powers[k]), tile)
        return [tile * np.float32(f) for f in factors]

    up = going_up(nz)[nz - cut :]
    down = going_down(nz)[:cut]
    ups = tiles(up[:8] / up[0], up[::8])
    ups[-1] = jnp.where(row == 7, np.float32(up[-1]), ups[-1])
    steady = down[8:16] / down[8]
    downs = tiles(steady, [down[8] / RHO**8] + list(down[8::8]))
    downs[0] = jnp.where(row == 0, np.float32(down[0]), downs[0])
    return jnp.concatenate(ups, 0), jnp.concatenate(downs, 0)


def edges_call(velocity):
    _, nx, ny, nz = velocity.shape
    sub = LANES // ny
    chunks = nx // sub
    nq = len(Z_SUMS) + len(CELLS)
    cut_x = min(REACH, nx)
    cut = min(REACH, nz)
    group = 8
    parts = 8
    part = nx // parts

    def body(v_hbm, xu_ref, xd_ref, zu_ref, zd_ref, v_ref, sems):
        copies = [
            pltpu.make_async_copy(
                v_hbm.at[:, pl.ds(p * part, part)], v_ref.at[:, pl.ds(p * part, part)], sems.at[p]
            )
            for p in range(parts)
        ]
        for copy in copies:
            copy.start()
        weight_up, weight_down = z_weights(nz, cut)

        def x_rows(acc, weights, rows):
            for i in rows:
                vals = {c: v_ref[COMP[c], i] for c in CELLS}
                for q, name in enumerate(X_SUMS):
                    term = product(vals, name) * np.float32(weights[i])
                    acc[q] = term if acc[q] is None else acc[q] + term

        ups = [None] * len(X_SUMS)
        downs = [None] * len(X_SUMS)
        rows = {}
        for p in range(parts):
            copies[p].wait()
            for s in range(p * part // sub, (p + 1) * part // sub):
                t = {c: v_ref[COMP[c], s * sub : (s + 1) * sub].reshape(LANES, nz).T for c in CELLS}
                for q, name in enumerate(Z_SUMS):
                    f = product(t, name)
                    up = jnp.sum(f[nz - cut :] * weight_up, axis=0, keepdims=True)
                    down = jnp.sum(f[:cut] * weight_down, axis=0, keepdims=True)
                    rows.setdefault(q, []).append((up, down))
                for q, name in enumerate(CELLS):
                    rows.setdefault(len(Z_SUMS) + q, []).append((t[name][nz - 1 : nz], t[name][0:1]))
                if (s + 1) % group == 0:
                    at = s + 1 - group
                    for q, pairs in rows.items():
                        zu_ref[q, at : at + group] = jnp.concatenate([r[0] for r in pairs], 0)
                        zd_ref[q, at : at + group] = jnp.concatenate([r[1] for r in pairs], 0)
                    rows = {}
            here = range(p * part, (p + 1) * part)
            x_rows(downs, going_down(nx), [i for i in here if i < cut_x])
            x_rows(ups, going_up(nx), [i for i in here if i >= nx - cut_x])
        for q in range(len(X_SUMS)):
            xu_ref[q] = ups[q]
            xd_ref[q] = downs[q]
        for q in range(len(CELLS)):
            xu_ref[len(X_SUMS) + q] = v_ref[q, nx - 1]
            xd_ref[len(X_SUMS) + q] = v_ref[q, 0]

    xs = jax.ShapeDtypeStruct((nq, ny, nz), F32)
    zs = jax.ShapeDtypeStruct((nq, chunks, LANES), F32)
    return pl.pallas_call(
        body,
        in_specs=[HBM],
        out_specs=[VMEM] * 5,
        out_shape=[xs, xs, zs, zs, jax.ShapeDtypeStruct(velocity.shape, F32)],
        scratch_shapes=[pltpu.SemaphoreType.DMA((parts,))],
        compiler_params=params(),
        name="edges",
        cost_estimate=cost(6, nx * ny * nz),
    )(pltpu.with_memory_space_constraint(velocity, pltpu.HBM))


def x_derivatives(read, write, scratch, nx, rims, pieces=1, done=None):
    unroll = 8
    half = nx // 2
    blocks = half // unroll
    fields = range(len(rims))
    grown = [KAPPA * RHO ** -(k + 1) for k in range(unroll)]
    power = [RHO**k for k in range(unroll + 1)]

    def sweep(first):
        def step(b, carry):
            out = []
            lows = (0 if first else half) + b * unroll
            highs = (nx if first else half) - 1 - b * unroll
            for f in fields:
                low, before, here, high, after, there = carry[f]
                _, cell_before, _, cell_after = rims[f]
                for k in range(unroll):
                    i = lows + k
                    part = low if k == 0 else power[k] * low
                    edge = here - before
                    if first:
                        nxt = read(f, i + 1)
                        scratch(f)[i] = part
                    else:
                        if k == unroll - 1:
                            inside = read(f, jnp.minimum(i + 1, nx - 1))
                            nxt = jnp.where(b == blocks - 1, cell_after, inside)
                        else:
                            nxt = read(f, i + 1)
                        write(f, i, scratch(f)[i] + (part + NEAR * (nxt - before)))
                    low = low + grown[k] * edge
                    before, here = here, nxt

                    i = highs - k
                    part = high if k == 0 else power[k] * high
                    edge = after - there
                    if first:
                        nxt = read(f, i - 1)
                        scratch(f)[i] = part
                    else:
                        if k == unroll - 1:
                            inside = read(f, jnp.maximum(i - 1, 0))
                            nxt = jnp.where(b == blocks - 1, cell_before, inside)
                        else:
                            nxt = read(f, i - 1)
                        write(f, i, scratch(f)[i] + (part + NEAR * (after - nxt)))
                    high = high + grown[k] * edge
                    after, there = there, nxt
                out.append((power[unroll] * low, before, here, power[unroll] * high, after, there))
            return tuple(out)

        return step

    carry = tuple(
        (TAIL * sum_before, cell_before, read(f, 0), TAIL * sum_after, cell_after, read(f, nx - 1))
        for f, (sum_before, cell_before, sum_after, cell_after) in enumerate(rims)
    )
    carry = lax.fori_loop(0, blocks, sweep(True), carry)
    for p in range(pieces):
        lo, hi = p * blocks // pieces, (p + 1) * blocks // pieces
        carry = lax.fori_loop(lo, hi, sweep(False), carry)
        if done is not None:
            done(half + lo * unroll, (hi - lo) * unroll)
            done(half - hi * unroll, (hi - lo) * unroll)


class Outbox:
    def __init__(self, sems):
        self.sems, self.copies = sems, []

    def send(self, src, dst):
        copy = pltpu.make_async_copy(src, dst, self.sems.at[len(self.copies)])
        copy.start()
        self.copies.append(copy)

    def wait(self):
        for copy in self.copies:
            copy.wait()


def params(mib=8):
    return pltpu.CompilerParams(vmem_limit_bytes=mib * 2**20)


def cost(fields, size):
    return pl.CostEstimate(flops=fields * size * 512, transcendentals=0, bytes_accessed=fields * size * 8)


def inner_z(velocity, inner):
    _, nx, ny, nz = velocity.shape
    rows = nx * ny

    def body(v_ref, m_ref, w_out, u_out, v_out, *c_outs):
        outs = (u_out, v_out, w_out) + c_outs
        keep = lax.broadcasted_iota(jnp.int32, (rows, LANES), 1) < LANES - 1
        both = jnp.concatenate([m_ref[0], m_ref[0]], 0)
        w = v_ref[2].reshape(rows, nz)
        for c in range(6):
            f = v_ref[c % 3].reshape(rows, nz)
            if c >= 3:
                f = f * w
            e = jnp.where(keep, pltpu.roll(f, LANES - 1, 1) - f, 0.0)
            hi, lo = split2(e)
            g = dot(jnp.concatenate([hi, lo], 1), both) + dot(hi, m_ref[1])
            outs[c][...] = g.reshape(nx, ny, nz)

    return pl.pallas_call(
        body,
        in_specs=[VMEM, VMEM],
        out_specs=[VMEM] * 6,
        out_shape=[jax.ShapeDtypeStruct(velocity.shape[1:], F32)] * 6,
        compiler_params=params(),
        name="inner_z",
        cost_estimate=cost(6, nx * ny * nz),
    )(velocity, inner)


def slopes_first(velocity, inner, x_halo, z_halo, rims):
    _, nx, ny, nz = velocity.shape
    sub = LANES // ny
    chunks = nx // sub
    rows = nx * ny

    def body(v_ref, i_ref, xl, xr, zl, zr, own_l, own_r, m_ref, gu, gw, tx, tz, st, px, pz, scratch, rim):
        used = 12 * len(Z_SUMS)
        rim[:, used:, :] = jnp.zeros((chunks, LANES - used, LANES), F32)
        for f in range(6):
            cells = [r[6 + f % 3] for r in (zl, own_l, own_r, zr)]
            if f >= 3:
                cells = [c * r[8] for c, r in zip(cells, (zl, own_l, own_r, zr))]
            terms = [cells[1] - cells[0], zl[f], cells[3] - cells[2], zr[f]]
            for q, term in enumerate(terms):
                hi = term.astype(BF16).astype(F32)
                lo = (term - hi).astype(BF16).astype(F32)
                rim[:, 12 * f + q, :] = hi
                rim[:, 12 * f + 4 + q, :] = lo
                rim[:, 12 * f + 8 + q, :] = hi
        for c in range(chunks):
            st[c * LANES : (c + 1) * LANES] = rim[c].T.astype(BF16)

        g = i_ref[...].reshape(rows, nz) + dot(st[...], m_ref[2])
        gw[...] = g.reshape(nx, ny, nz)

        def write_x(_, i, g):
            gu[i] = g

        rims_x = [(xl[0], xl[6], xr[0], xr[6])]
        x_derivatives(lambda _, i: v_ref[0, i], write_x, lambda _: scratch, nx, rims_x)

        zero = jnp.zeros((ny, nz), F32)
        ways = 4

        def add(b, carry):
            out = []
            for k, (total, moment) in enumerate(carry):
                for n in range(2):
                    i = b * 2 * ways + 2 * k + n
                    g = gw[i]
                    total = total + g
                    moment = moment + (i.astype(F32) - 0.5 * (nx - 1)) * g
                out.append((total, moment))
            return tuple(out)

        got = lax.fori_loop(0, nx // (2 * ways), add, ((zero, zero),) * ways)
        bits, centre, start = place("gx", nx)
        total = (got[0][0] + got[1][0]) + (got[2][0] + got[3][0])
        tx[0] = total
        tx[1] = (got[0][1] + got[1][1]) + (got[2][1] + got[3][1]) + centre * total
        for k, value in enumerate([*bits, start]):
            px[k] = jnp.full((ny, nz), value, F32)

        at = lax.broadcasted_iota(jnp.int32, (nz, LANES), 0).astype(F32) - 0.5 * (nz - 1)
        totals, moments = [], []
        for c in range(chunks):
            t = gu[c * sub : (c + 1) * sub].reshape(LANES, nz).T
            totals.append(jnp.sum(t, axis=0, keepdims=True))
            moments.append(jnp.sum(t * at, axis=0, keepdims=True))
        bits, centre, start = place("gz", nz)
        total = jnp.concatenate(totals, 0)
        tz[0] = total
        tz[1] = jnp.concatenate(moments, 0) + centre * total
        for k, value in enumerate([*bits, start]):
            pz[k] = jnp.full((chunks, LANES), value, F32)

    one = jax.ShapeDtypeStruct(velocity.shape[1:], F32)
    sx = jax.ShapeDtypeStruct((2, ny, nz), F32)
    sz = jax.ShapeDtypeStruct((2, chunks, LANES), F32)
    st = jax.ShapeDtypeStruct((rows, LANES), BF16)
    small = [*x_halo, *z_halo, rims]
    steps_x = sum(len(below_tests(level)) for level in LEVELS["gx"])
    steps_z = sum(len(below_tests(level)) for level in LEVELS["gz"])
    px = jax.ShapeDtypeStruct((steps_x + 1, ny, nz), F32)
    pz = jax.ShapeDtypeStruct((steps_z + 1, chunks, LANES), F32)
    outs = [one, one, sx, sz, st, px, pz]
    return pl.pallas_call(
        body,
        in_specs=[VMEM] * (2 + len(small)),
        out_specs=[VMEM] * len(outs),
        out_shape=outs,
        scratch_shapes=[pltpu.VMEM((nx, ny, nz), F32), pltpu.VMEM((chunks, LANES, LANES), F32)],
        compiler_params=params(),
        name="slopes_first",
        cost_estimate=cost(2, nx * ny * nz),
    )(velocity, inner, *small)


def slopes_rest(velocity, inner_u, inner_v, x_halo, st, rims, gw):
    _, nx, ny, nz = velocity.shape
    rows = nx * ny
    parts = 2

    def body(v_ref, iu_ref, iv_ref, xl, xr, st_ref, m_ref, gw_ref, gv, gx, out, s0, s1, made, sems):
        box = Outbox(sems)
        box.send(gw_ref, out.at[2])
        for c, i_ref in enumerate((iu_ref, iv_ref)):
            for p in range(parts):
                at = pl.ds(p * nx // parts, nx // parts)
                local = i_ref[at].reshape(rows // parts, nz)
                g = local + dot(st_ref[pl.ds(p * rows // parts, rows // parts)], m_ref[c])
                made[c, at] = g.reshape(nx // parts, ny, nz)
                box.send(made.at[c, at], out.at[c, at])

        def write(f, i, g):
            (gv, gx)[f][i] = g

        x_derivatives(
            lambda f, i: v_ref[1 + f, i],
            write,
            lambda f: (s0, s1)[f],
            nx,
            [(xl[c], xl[6 + c], xr[c], xr[6 + c]) for c in (1, 2)],
        )
        box.wait()

    one = jax.ShapeDtypeStruct((nx, ny, nz), F32)
    return pl.pallas_call(
        body,
        in_specs=[VMEM] * 8,
        out_specs=[VMEM, VMEM, ANY],
        out_shape=[one, one, jax.ShapeDtypeStruct(velocity.shape, F32)],
        scratch_shapes=[
            pltpu.VMEM((nx, ny, nz), F32),
            pltpu.VMEM((nx, ny, nz), F32),
            pltpu.VMEM((2, nx, ny, nz), F32),
            pltpu.SemaphoreType.DMA((8,)),
        ],
        compiler_params=params(),
        name="slopes_rest",
        cost_estimate=cost(3, nx * ny * nz),
    )(velocity, inner_u, inner_v, *x_halo, st, rims, gw)


def prepare(inner, st, rims, slopes, sums):
    nx, ny, nz = slopes[0].shape
    rows = nx * ny

    def body(*refs):
        i_refs, g_refs, st_ref, m_ref, t_ref = refs[:3], refs[3:6], *refs[6:9]
        *c_refs, local, gx, sems = refs[9:]
        box = Outbox(sems)
        for c in range(3):
            box.send(g_refs[c], gx.at[c])
        hi, mid, lo = split3(g_refs[0][...].reshape(rows, nz))
        g = dot(jnp.concatenate([hi, mid], 1), t_ref[0]) + dot(lo, t_ref[1, :LANES])
        local[...] = g.reshape(nx, ny, nz)
        for c in range(3):
            g = i_refs[c][...].reshape(rows, nz) + dot(st_ref[...], m_ref[3 + c])
            c_refs[c][...] = g.reshape(nx, ny, nz)
        box.wait()

    one = jax.ShapeDtypeStruct((nx, ny, nz), F32)
    *parts, local, gx = pl.pallas_call(
        body,
        in_specs=[VMEM] * 9,
        out_specs=[VMEM] * 4 + [ANY],
        out_shape=[one] * 4 + [jax.ShapeDtypeStruct((3, nx, ny, nz), F32)],
        scratch_shapes=[pltpu.SemaphoreType.DMA((4,))],
        compiler_params=params(),
        name="prepare",
        cost_estimate=cost(3, nx * ny * nz),
    )(*inner, *slopes, st, rims, sums)
    return parts, local, gx


def divergence(velocity, along_z, x_halo):
    _, nx, ny, nz = velocity.shape
    comps = range(3)

    def body(v_ref, xl, xr, *rest):
        z_refs = rest[:3]
        out, s0, s1, s2, m0, m1, m2, sems = rest[3:]
        made = (m0, m1, m2)
        box = Outbox(sems)

        def write(c, i, g):
            made[c][i] = z_refs[c][i] + g

        def done(start, size):
            at = pl.ds(start, size)
            for c in comps:
                box.send(made[c].at[at], out.at[c, at])

        x_derivatives(
            lambda c, i: v_ref[0, i] * v_ref[c, i],
            write,
            lambda c: (s0, s1, s2)[c],
            nx,
            [(xl[3 + c], xl[6] * xl[6 + c], xr[3 + c], xr[6] * xr[6 + c]) for c in comps],
            4,
            done,
        )
        box.wait()

    return pl.pallas_call(
        body,
        in_specs=[VMEM] * 6,
        out_specs=ANY,
        out_shape=jax.ShapeDtypeStruct(velocity.shape, F32),
        scratch_shapes=[pltpu.VMEM((nx, ny, nz), F32)] * 6 + [pltpu.SemaphoreType.DMA((32,))],
        compiler_params=params(12),
        name="divergence",
        cost_estimate=cost(6, nx * ny * nz),
    )(velocity, *x_halo, *along_z)


def rebuild(local, gw, x_terms, z_terms, mats, total_x, total_z):
    nx, ny, nz = gw.shape
    sub = LANES // ny
    chunks = nx // sub
    rows = nx * ny
    parts = 4
    scale_x = -1.0 / math.sqrt(total_x)
    scale_z = -1.0 / math.sqrt(total_z)

    def body(l_ref, w_ref, xt, zt, m_ref, out, rim, made, sems):
        box = Outbox(sems)
        mean = xt[1]

        def along_x(b, acc):
            for k in range(8):
                i = b * 8 + k
                g = w_ref[i]
                made[0, i] = scale_x * (acc + 0.5 * g)
                acc = acc + (g - mean)
            return acc

        acc = xt[0]
        for p in range(parts):
            acc = lax.fori_loop(p * nx // parts // 8, (p + 1) * nx // parts // 8, along_x, acc)
            at = pl.ds(p * nx // parts, nx // parts)
            box.send(made.at[0, at], out.at[0, at])
        rim[:, 6:, :] = jnp.zeros((chunks, LANES - 6, LANES), F32)
        for q in range(2):
            for p, part in enumerate(split3(zt[q])):
                rim[:, 3 * q + p, :] = part.astype(F32)
        for p in range(parts):
            at = pl.ds(p * nx // parts, nx // parts)
            here = range(p * chunks // parts, (p + 1) * chunks // parts)
            st = jnp.concatenate([rim[c].T.astype(BF16) for c in here], 0)
            g = l_ref[at].reshape(rows // parts, nz) + dot(st, m_ref[1, LANES:])
            made[1, at] = (scale_z * g).reshape(nx // parts, ny, nz)
            box.send(made.at[1, at], out.at[1, at])
        box.wait()

    shape = (2,) + gw.shape
    return pl.pallas_call(
        body,
        in_specs=[VMEM] * 5,
        out_specs=ANY,
        out_shape=jax.ShapeDtypeStruct(shape, F32),
        scratch_shapes=[
            pltpu.VMEM((chunks, LANES, LANES), F32),
            pltpu.VMEM(shape, F32),
            pltpu.SemaphoreType.DMA((16,)),
        ],
        compiler_params=params(),
        name="rebuild",
        cost_estimate=cost(2, nx * ny * nz),
    )(local, gw, x_terms, z_terms, mats)


def swap(axis, up, down):
    n = lax.axis_size(axis)
    before = lax.ppermute(up, axis, [(i, (i + 1) % n) for i in range(n)])
    after = lax.ppermute(down, axis, [((i + 1) % n, i) for i in range(n)])
    return before, after


LEVELS = {
    "gx": [(2, 1, False), (2, 2, False), (4, 2, True)],
    "gz": [(4, 1, False), (2, 4, False), (4, 4, True)],
}
ROUNDS = [(("gx", "gz"), "rest"), (("gx", "gz"), "prepare"), (("gx", "gz"), "flux")]


def shifts(level):
    count, _, mirror = level
    if mirror:
        return [lambda own: count - 1 - 2 * own]
    order = sorted(range(1, count), key=lambda k: min(k, count - k))
    return [lambda own, k=k: (own + k) % count - own for k in order]


def below_tests(level):
    count, _, mirror = level
    if mirror:
        return [count // 2]
    return sorted(range(1, count), key=lambda k: min(k, count - k))


def exchange(axis, terms, level):
    n = lax.axis_size(axis)
    count, stride, _ = level
    parts = []
    for shift in shifts(level):
        pairs = [(i, i + shift((i // stride) % count) * stride) for i in range(n)]
        parts.append(lax.ppermute(terms, axis, pairs))
    return parts


def combine(terms, before, parts, below):
    for mask, part in zip(below, parts):
        before = before + mask * part[0]
        terms = terms + part
    return terms, before


def place(axis, cells):
    n = lax.axis_size(axis)
    mine = lax.axis_index(axis)
    below = []
    for level in LEVELS[axis]:
        own = mine // level[1] % level[0]
        below += [(own >= least).astype(F32) for least in below_tests(level)]
    start = (mine * cells).astype(F32)
    centre = start + (0.5 * (cells - 1) - 0.5 * (n * cells - 1))
    return below, centre, (start + 0.5) * (1.0 / (n * cells))


def below_of(axis, spot, at):
    skip = sum(len(below_tests(level)) for level in LEVELS[axis][:at])
    return [spot[skip + k] for k in range(len(below_tests(LEVELS[axis][at])))]


def line_terms(terms, before, start, total_len):
    mean = terms[0] / total_len
    offset = before - start * terms[0] + terms[1] / total_len
    return jnp.stack([offset, mean])


def body(velocity):
    _, nx, ny, nz = velocity.shape
    size_x = lax.axis_size("gx")
    size_z = lax.axis_size("gz")
    total_x = nx * size_x
    total_z = nz * size_z
    inner_mats = jnp.asarray(z_inner())
    rims = jnp.asarray(z_rims(len(Z_SUMS)))
    sums = jnp.asarray(sum_matrices())

    xu, xd, zu, zd, vel = edges_call(velocity)
    z_halo = (*swap("gz", zu, zd), zd, zu)
    x_halo = swap("gx", xu, xd)
    in_w, in_u, in_v, *in_c = inner_z(vel, inner_mats)
    gu, gw, tx, tz, st, spot_x, spot_z = slopes_first(vel, in_w, x_halo, z_halo, rims)
    bx = jnp.zeros_like(tx[0])
    bz = jnp.zeros_like(tz[0])

    terms = {"gx": (tx, bx), "gz": (tz, bz)}
    spots = {"gx": spot_x, "gz": spot_z}
    done = {"gx": 0, "gz": 0}
    for axes, filler in ROUNDS:
        parts = {axis: exchange(axis, terms[axis][0], LEVELS[axis][done[axis]]) for axis in axes}
        made = ()
        if filler == "rest":
            made = slopes_rest(vel, in_u, in_v, x_halo, st, rims, gw)
        elif filler == "flux":
            made = divergence(vel, in_c, x_halo)
        elif filler == "prepare":
            made = prepare(in_c, st, rims, (gu, gv, gq), sums)
        if filler:
            parts, made = lax.optimization_barrier((parts, made))
        if filler == "rest":
            gv, gq, grad_z = made
        elif filler == "prepare":
            in_c, local, grad_x = made
        elif filler == "flux":
            convect = made
        for axis in axes:
            below = below_of(axis, spots[axis], done[axis])
            terms[axis] = combine(*terms[axis], parts[axis], below)
            done[axis] += 1
    (tx, bx), (tz, bz) = terms["gx"], terms["gz"]
    rebuilt = rebuild(
        local,
        gw,
        line_terms(tx, bx, spot_x[-1], total_x),
        line_terms(tz, bz, spot_z[-1], total_z),
        sums,
        total_x,
        total_z,
    )
    return (grad_x, grad_z, convect, rebuilt)


def solution(mesh):
    spec = P(None, "gx", None, "gz")
    return jax.shard_map(
        body, mesh=mesh, in_specs=(spec,), out_specs=(spec,) * 4, check_vma=False
    )
```

```python
import math

import jax
import jax.numpy as jnp
import numpy as np
from jax import lax
from jax.experimental import pallas as pl
from jax.experimental.pallas import tpu as pltpu
from jax.sharding import PartitionSpec as P

ALPHA = 1.0 / 3.0
COEF_A = 14.0 / 9.0
COEF_B = 1.0 / 9.0
LANES = 128
F32 = jnp.float32
VMEM = pl.BlockSpec(memory_space=pltpu.VMEM)
HBM = pl.BlockSpec(memory_space=pltpu.HBM)
ANY = pl.BlockSpec(memory_space=pl.ANY)
BF16 = jnp.bfloat16

RHO = (-1.0 + math.sqrt(1.0 - 4.0 * ALPHA * ALPHA)) / (2.0 * ALPHA)


def kernel_weights():
    reach = 400
    k = np.arange(-reach, reach + 1)
    green = RHO ** np.abs(k).astype(np.float64) / math.sqrt(1.0 - 4.0 * ALPHA * ALPHA)

    def shifted(s):
        out = np.zeros_like(green)
        if s >= 0:
            out[s:] = green[: len(green) - s]
        else:
            out[:s] = green[-s:]
        return out

    direct = 0.5 * COEF_A * (shifted(-1) - shifted(1)) + 0.25 * COEF_B * (shifted(-2) - shifted(2))
    total = np.concatenate([[0.0], np.cumsum(direct)])
    return {m: total[m + reach] for m in range(-2, 4)}


_W = kernel_weights()
NEAR = _W[1]
TAIL = _W[2] / RHO**2
KAPPA = TAIL * RHO * RHO
TOGETHER = 16
REACH = 96


def h_of(m):
    m = np.asarray(m)
    m = np.where(m <= 0, 1 - m, m)
    return np.where(m == 1, NEAR, TAIL * RHO ** m.astype(np.float64))


def split_np(x):
    hi = x.astype(BF16)
    lo = (x - hi.astype(np.float64)).astype(BF16)
    return hi, lo


def going_up(length):
    j = np.arange(length)
    w = (RHO - 1.0) * RHO ** (length - j).astype(np.float64)
    w[-1] = RHO**2
    return w


def going_down(length):
    return going_up(length)[::-1] * -1.0


def z_inner():
    j = np.arange(LANES)
    inner = h_of(j[None, :] - j[:, None])
    inner[LANES - 1] = 0.0
    hi, lo = split_np(inner)
    return np.stack([hi, lo])


def z_rims(fields):
    j = np.arange(LANES)
    rim = np.stack(
        [
            h_of(j + 1),
            TAIL * RHO ** j.astype(np.float64),
            h_of(LANES - j),
            TAIL * RHO ** (LANES - 1 - j).astype(np.float64),
        ]
    )
    hi, lo = split_np(rim)
    out = np.zeros((fields, LANES, LANES), BF16)
    for f in range(fields):
        out[f, 12 * f : 12 * f + 12] = np.concatenate([hi, hi, lo], 0)
    return out


def sum_matrices():
    j = np.arange(LANES)
    lower = (j[:, None] < j[None, :]) + 0.5 * (j[:, None] == j[None, :])
    ones = np.ones((3, LANES))
    slope = -np.broadcast_to(j, (3, LANES))
    pad = np.zeros((LANES - 6, LANES))
    first = np.concatenate([lower, lower], 0)
    second = np.concatenate([lower, ones, slope, pad], 0)
    return np.stack([first, second]).astype(BF16)


def split2(x):
    hi = x.astype(BF16)
    return hi, (x - hi.astype(F32)).astype(BF16)


def split3(x):
    hi = x.astype(BF16)
    rest = x - hi.astype(F32)
    mid = rest.astype(BF16)
    return hi, mid, (rest - mid.astype(F32)).astype(BF16)


def dot(a, b):
    return lax.dot_general(a, b, (((1,), (0,)), ((), ())), preferred_element_type=F32)


def product(values, name):
    out = values[name[0]]
    for c in name[1:]:
        out = out * values[c]
    return out


COMP = {"u": 0, "v": 1, "w": 2}


X_SUMS = ["u", "v", "w", "uu", "uv", "uw"]
Z_SUMS = ["u", "v", "w", "wu", "wv", "ww"]
CELLS = ["u", "v", "w"]


def z_weights(nz, cut):
    row = lax.broadcasted_iota(jnp.int32, (8, LANES), 0)

    def tiles(powers, factors):
        tile = jnp.zeros((8, LANES), F32)
        for k in range(8):
            tile = jnp.where(row == k, np.float32(powers[k]), tile)
        return [tile * np.float32(f) for f in factors]

    up = going_up(nz)[nz - cut :]
    down = going_down(nz)[:cut]
    ups = tiles(up[:8] / up[0], up[::8])
    ups[-1] = jnp.where(row == 7, np.float32(up[-1]), ups[-1])
    steady = down[8:16] / down[8]
    downs = tiles(steady, [down[8] / RHO**8] + list(down[8::8]))
    downs[0] = jnp.where(row == 0, np.float32(down[0]), downs[0])
    return jnp.concatenate(ups, 0), jnp.concatenate(downs, 0)


def edges_call(velocity):
    _, nx, ny, nz = velocity.shape
    sub = LANES // ny
    chunks = nx // sub
    nq = len(Z_SUMS) + len(CELLS)
    cut_x = min(REACH, nx)
    cut = min(REACH, nz)
    group = 8
    parts = 4
    part = nx // parts

    def body(v_hbm, xu_ref, xd_ref, zu_ref, zd_ref, v_ref, sems):
        copies = [
            pltpu.make_async_copy(
                v_hbm.at[:, pl.ds(p * part, part)], v_ref.at[:, pl.ds(p * part, part)], sems.at[p]
            )
            for p in range(parts)
        ]
        for copy in copies:
            copy.start()
        weight_up, weight_down = z_weights(nz, cut)

        def x_rows(acc, weights, rows):
            for i in rows:
                vals = {c: v_ref[COMP[c], i] for c in CELLS}
                for q, name in enumerate(X_SUMS):
                    term = product(vals, name) * np.float32(weights[i])
                    acc[q] = term if acc[q] is None else acc[q] + term

        ups = [None] * len(X_SUMS)
        downs = [None] * len(X_SUMS)
        rows = {}
        for p in range(parts):
            copies[p].wait()
            for s in range(p * part // sub, (p + 1) * part // sub):
                t = {c: v_ref[COMP[c], s * sub : (s + 1) * sub].reshape(LANES, nz).T for c in CELLS}
                for q, name in enumerate(Z_SUMS):
                    f = product(t, name)
                    up = jnp.sum(f[nz - cut :] * weight_up, axis=0, keepdims=True)
                    down = jnp.sum(f[:cut] * weight_down, axis=0, keepdims=True)
                    rows.setdefault(q, []).append((up, down))
                for q, name in enumerate(CELLS):
                    rows.setdefault(len(Z_SUMS) + q, []).append((t[name][nz - 1 : nz], t[name][0:1]))
                if (s + 1) % group == 0:
                    at = s + 1 - group
                    for q, pairs in rows.items():
                        zu_ref[q, at : at + group] = jnp.concatenate([r[0] for r in pairs], 0)
                        zd_ref[q, at : at + group] = jnp.concatenate([r[1] for r in pairs], 0)
                    rows = {}
            here = range(p * part, (p + 1) * part)
            x_rows(downs, going_down(nx), [i for i in here if i < cut_x])
            x_rows(ups, going_up(nx), [i for i in here if i >= nx - cut_x])
        for q in range(len(X_SUMS)):
            xu_ref[q] = ups[q]
            xd_ref[q] = downs[q]
        for q in range(len(CELLS)):
            xu_ref[len(X_SUMS) + q] = v_ref[q, nx - 1]
            xd_ref[len(X_SUMS) + q] = v_ref[q, 0]

    xs = jax.ShapeDtypeStruct((nq, ny, nz), F32)
    zs = jax.ShapeDtypeStruct((nq, chunks, LANES), F32)
    return pl.pallas_call(
        body,
        in_specs=[HBM],
        out_specs=[VMEM] * 5,
        out_shape=[xs, xs, zs, zs, jax.ShapeDtypeStruct(velocity.shape, F32)],
        scratch_shapes=[pltpu.SemaphoreType.DMA((parts,))],
        compiler_params=params(),
        name="edges",
        cost_estimate=cost(6, nx * ny * nz),
    )(pltpu.with_memory_space_constraint(velocity, pltpu.HBM))


def x_derivatives(read, write, scratch, nx, rims, pieces=1, done=None):
    unroll = 8
    half = nx // 2
    blocks = half // unroll
    fields = range(len(rims))
    grown = [KAPPA * RHO ** -(k + 1) for k in range(unroll)]
    power = [RHO**k for k in range(unroll + 1)]

    def sweep(first):
        def step(b, carry):
            out = []
            lows = (0 if first else half) + b * unroll
            highs = (nx if first else half) - 1 - b * unroll
            for f in fields:
                low, before, here, high, after, there = carry[f]
                _, cell_before, _, cell_after = rims[f]
                for k in range(unroll):
                    i = lows + k
                    part = low if k == 0 else power[k] * low
                    edge = here - before
                    if first:
                        nxt = read(f, i + 1)
                        scratch(f)[i] = part
                    else:
                        if k == unroll - 1:
                            inside = read(f, jnp.minimum(i + 1, nx - 1))
                            nxt = jnp.where(b == blocks - 1, cell_after, inside)
                        else:
                            nxt = read(f, i + 1)
                        write(f, i, scratch(f)[i] + (part + NEAR * (nxt - before)))
                    low = low + grown[k] * edge
                    before, here = here, nxt

                    i = highs - k
                    part = high if k == 0 else power[k] * high
                    edge = after - there
                    if first:
                        nxt = read(f, i - 1)
                        scratch(f)[i] = part
                    else:
                        if k == unroll - 1:
                            inside = read(f, jnp.maximum(i - 1, 0))
                            nxt = jnp.where(b == blocks - 1, cell_before, inside)
                        else:
                            nxt = read(f, i - 1)
                        write(f, i, scratch(f)[i] + (part + NEAR * (after - nxt)))
                    high = high + grown[k] * edge
                    after, there = there, nxt
                out.append((power[unroll] * low, before, here, power[unroll] * high, after, there))
            return tuple(out)

        return step

    carry = tuple(
        (TAIL * sum_before, cell_before, read(f, 0), TAIL * sum_after, cell_after, read(f, nx - 1))
        for f, (sum_before, cell_before, sum_after, cell_after) in enumerate(rims)
    )
    carry = lax.fori_loop(0, blocks, sweep(True), carry)
    for p in range(pieces):
        lo, hi = p * blocks // pieces, (p + 1) * blocks // pieces
        carry = lax.fori_loop(lo, hi, sweep(False), carry)
        if done is not None:
            done(half + lo * unroll, (hi - lo) * unroll)
            done(half - hi * unroll, (hi - lo) * unroll)


def rim_terms(rim, base, field, zl, zr, own_l, own_r):
    cells = [r[6 + field % 3] for r in (zl, own_l, own_r, zr)]
    if field >= 3:
        cells = [c * r[8] for c, r in zip(cells, (zl, own_l, own_r, zr))]
    terms = [cells[1] - cells[0], zl[field], cells[3] - cells[2], zr[field]]
    for q, term in enumerate(terms):
        hi = term.astype(BF16).astype(F32)
        lo = (term - hi).astype(BF16).astype(F32)
        rim[:, base + q, :] = hi
        rim[:, base + 4 + q, :] = lo
        rim[:, base + 8 + q, :] = hi


class Outbox:
    def __init__(self, sems):
        self.sems, self.copies = sems, []

    def send(self, src, dst):
        copy = pltpu.make_async_copy(src, dst, self.sems.at[len(self.copies)])
        copy.start()
        self.copies.append(copy)

    def wait(self):
        for copy in self.copies:
            copy.wait()


def params(mib=8):
    return pltpu.CompilerParams(vmem_limit_bytes=mib * 2**20)


def cost(fields, size):
    return pl.CostEstimate(flops=fields * size * 512, transcendentals=0, bytes_accessed=fields * size * 8)


def inner_z(velocity, inner):
    _, nx, ny, nz = velocity.shape
    rows = nx * ny

    def body(v_ref, m_ref, w_out, u_out, v_out, *c_outs):
        outs = (u_out, v_out, w_out) + c_outs
        keep = lax.broadcasted_iota(jnp.int32, (rows, LANES), 1) < LANES - 1
        both = jnp.concatenate([m_ref[0], m_ref[0]], 0)
        w = v_ref[2].reshape(rows, nz)
        for c in range(6):
            f = v_ref[c % 3].reshape(rows, nz)
            if c >= 3:
                f = f * w
            e = jnp.where(keep, pltpu.roll(f, LANES - 1, 1) - f, 0.0)
            hi, lo = split2(e)
            g = dot(jnp.concatenate([hi, lo], 1), both) + dot(hi, m_ref[1])
            outs[c][...] = g.reshape(nx, ny, nz)

    return pl.pallas_call(
        body,
        in_specs=[VMEM, VMEM],
        out_specs=[VMEM] * 6,
        out_shape=[jax.ShapeDtypeStruct(velocity.shape[1:], F32)] * 6,
        compiler_params=params(),
        name="inner_z",
        cost_estimate=cost(6, nx * ny * nz),
    )(velocity, inner)


def slopes_first(velocity, inner, x_halo, z_halo, rims):
    _, nx, ny, nz = velocity.shape
    sub = LANES // ny
    chunks = nx // sub
    rows = nx * ny

    def body(v_ref, i_ref, xl, xr, zl, zr, own_l, own_r, m_ref, gu, gw, tx, tz, px, pz, scratch, rim):
        rim[:, 12:, :] = jnp.zeros((chunks, 4, LANES), F32)
        rim_terms(rim, 0, 2, zl, zr, own_l, own_r)
        st = jnp.concatenate([rim[c].T.astype(BF16) for c in range(chunks)], 0)
        g = i_ref[...].reshape(rows, nz) + dot(st, m_ref[2, 24:40])
        gw[...] = g.reshape(nx, ny, nz)

        def write_x(_, i, g):
            gu[i] = g

        rims_x = [(xl[0], xl[6], xr[0], xr[6])]
        x_derivatives(lambda _, i: v_ref[0, i], write_x, lambda _: scratch, nx, rims_x)

        zero = jnp.zeros((ny, nz), F32)
        ways = 4

        def add(b, carry):
            out = []
            for k, (total, moment) in enumerate(carry):
                for n in range(2):
                    i = b * 2 * ways + 2 * k + n
                    g = gw[i]
                    total = total + g
                    moment = moment + (i.astype(F32) - 0.5 * (nx - 1)) * g
                out.append((total, moment))
            return tuple(out)

        got = lax.fori_loop(0, nx // (2 * ways), add, ((zero, zero),) * ways)
        bits, centre, start = place("gx", nx)
        total = (got[0][0] + got[1][0]) + (got[2][0] + got[3][0])
        tx[0] = total
        tx[1] = (got[0][1] + got[1][1]) + (got[2][1] + got[3][1]) + centre * total
        for k, value in enumerate([*bits, start]):
            px[k] = jnp.full((ny, nz), value, F32)

        at = lax.broadcasted_iota(jnp.int32, (nz, LANES), 0).astype(F32) - 0.5 * (nz - 1)
        totals, moments = [], []
        for c in range(chunks):
            t = gu[c * sub : (c + 1) * sub].reshape(LANES, nz).T
            totals.append(jnp.sum(t, axis=0, keepdims=True))
            moments.append(jnp.sum(t * at, axis=0, keepdims=True))
        bits, centre, start = place("gz", nz)
        total = jnp.concatenate(totals, 0)
        tz[0] = total
        tz[1] = jnp.concatenate(moments, 0) + centre * total
        for k, value in enumerate([*bits, start]):
            pz[k] = jnp.full((chunks, LANES), value, F32)

    one = jax.ShapeDtypeStruct(velocity.shape[1:], F32)
    sx = jax.ShapeDtypeStruct((2, ny, nz), F32)
    sz = jax.ShapeDtypeStruct((2, chunks, LANES), F32)
    small = [*x_halo, *z_halo, rims]
    steps_x = sum(len(below_tests(level)) for level in LEVELS["gx"])
    steps_z = sum(len(below_tests(level)) for level in LEVELS["gz"])
    px = jax.ShapeDtypeStruct((steps_x + 1, ny, nz), F32)
    pz = jax.ShapeDtypeStruct((steps_z + 1, chunks, LANES), F32)
    outs = [one, one, sx, sz, px, pz]
    return pl.pallas_call(
        body,
        in_specs=[VMEM] * (2 + len(small)),
        out_specs=[VMEM] * len(outs),
        out_shape=outs,
        scratch_shapes=[pltpu.VMEM((nx, ny, nz), F32), pltpu.VMEM((chunks, 16, LANES), F32)],
        compiler_params=params(),
        name="slopes_first",
        cost_estimate=cost(2, nx * ny * nz),
    )(velocity, inner, *small)


def slopes_rest(velocity, inner_u, inner_v, x_halo, z_halo, rims, gw):
    _, nx, ny, nz = velocity.shape
    rows = nx * ny
    parts = 2

    chunks = rows // LANES

    def body(*refs):
        v_ref, iu_ref, iv_ref, xl, xr, zl, zr, own_l, own_r, m_ref, gw_ref = refs[:11]
        gv, gx, st_ref, out, s0, s1, made, rim, sems = refs[11:]
        box = Outbox(sems)
        box.send(gw_ref, out.at[2])
        used = 12 * len(Z_SUMS)
        rim[:, 24:36, :] = jnp.zeros((chunks, 12, LANES), F32)
        rim[:, used:, :] = jnp.zeros((chunks, LANES - used, LANES), F32)
        for field in (0, 1, 3, 4, 5):
            rim_terms(rim, 12 * field, field, zl, zr, own_l, own_r)
        for c in range(chunks):
            st_ref[c * LANES : (c + 1) * LANES] = rim[c].T.astype(BF16)
        for c, i_ref in enumerate((iu_ref, iv_ref)):
            for p in range(parts):
                at = pl.ds(p * nx // parts, nx // parts)
                local = i_ref[at].reshape(rows // parts, nz)
                g = local + dot(st_ref[pl.ds(p * rows // parts, rows // parts)], m_ref[c])
                made[c, at] = g.reshape(nx // parts, ny, nz)
                box.send(made.at[c, at], out.at[c, at])

        def write(f, i, g):
            (gv, gx)[f][i] = g

        x_derivatives(
            lambda f, i: v_ref[1 + f, i],
            write,
            lambda f: (s0, s1)[f],
            nx,
            [(xl[c], xl[6 + c], xr[c], xr[6 + c]) for c in (1, 2)],
        )
        box.wait()

    one = jax.ShapeDtypeStruct((nx, ny, nz), F32)
    return pl.pallas_call(
        body,
        in_specs=[VMEM] * 11,
        out_specs=[VMEM, VMEM, VMEM, ANY],
        out_shape=[
            one,
            one,
            jax.ShapeDtypeStruct((rows, LANES), BF16),
            jax.ShapeDtypeStruct(velocity.shape, F32),
        ],
        scratch_shapes=[
            pltpu.VMEM((nx, ny, nz), F32),
            pltpu.VMEM((nx, ny, nz), F32),
            pltpu.VMEM((2, nx, ny, nz), F32),
            pltpu.VMEM((chunks, LANES, LANES), F32),
            pltpu.SemaphoreType.DMA((8,)),
        ],
        compiler_params=params(),
        name="slopes_rest",
        cost_estimate=cost(3, nx * ny * nz),
    )(velocity, inner_u, inner_v, *x_halo, *z_halo, rims, gw)


def prepare(inner, st, rims, slopes, sums):
    nx, ny, nz = slopes[0].shape
    rows = nx * ny

    def body(*refs):
        i_refs, g_refs, st_ref, m_ref, t_ref = refs[:3], refs[3:6], *refs[6:9]
        *c_refs, local, gx, sems = refs[9:]
        box = Outbox(sems)
        for c in range(3):
            box.send(g_refs[c], gx.at[c])
        hi, mid, lo = split3(g_refs[0][...].reshape(rows, nz))
        g = dot(jnp.concatenate([hi, mid], 1), t_ref[0]) + dot(lo, t_ref[1, :LANES])
        local[...] = g.reshape(nx, ny, nz)
        for c in range(3):
            g = i_refs[c][...].reshape(rows, nz) + dot(st_ref[...], m_ref[3 + c])
            c_refs[c][...] = g.reshape(nx, ny, nz)
        box.wait()

    one = jax.ShapeDtypeStruct((nx, ny, nz), F32)
    *parts, local, gx = pl.pallas_call(
        body,
        in_specs=[VMEM] * 9,
        out_specs=[VMEM] * 4 + [ANY],
        out_shape=[one] * 4 + [jax.ShapeDtypeStruct((3, nx, ny, nz), F32)],
        scratch_shapes=[pltpu.SemaphoreType.DMA((4,))],
        compiler_params=params(),
        name="prepare",
        cost_estimate=cost(3, nx * ny * nz),
    )(*inner, *slopes, st, rims, sums)
    return parts, local, gx


def divergence(velocity, along_z, x_halo):
    _, nx, ny, nz = velocity.shape
    comps = range(3)

    def body(v_ref, xl, xr, *rest):
        z_refs = rest[:3]
        out, s0, s1, s2, m0, m1, m2, sems = rest[3:]
        made = (m0, m1, m2)
        box = Outbox(sems)

        def write(c, i, g):
            made[c][i] = z_refs[c][i] + g

        def done(start, size):
            at = pl.ds(start, size)
            for c in comps:
                box.send(made[c].at[at], out.at[c, at])

        x_derivatives(
            lambda c, i: v_ref[0, i] * v_ref[c, i],
            write,
            lambda c: (s0, s1, s2)[c],
            nx,
            [(xl[3 + c], xl[6] * xl[6 + c], xr[3 + c], xr[6] * xr[6 + c]) for c in comps],
            4,
            done,
        )
        box.wait()

    return pl.pallas_call(
        body,
        in_specs=[VMEM] * 6,
        out_specs=ANY,
        out_shape=jax.ShapeDtypeStruct(velocity.shape, F32),
        scratch_shapes=[pltpu.VMEM((nx, ny, nz), F32)] * 6 + [pltpu.SemaphoreType.DMA((32,))],
        compiler_params=params(12),
        name="divergence",
        cost_estimate=cost(6, nx * ny * nz),
    )(velocity, *x_halo, *along_z)


def rebuild(local, gw, x_terms, z_terms, mats, total_x, total_z):
    nx, ny, nz = gw.shape
    sub = LANES // ny
    chunks = nx // sub
    rows = nx * ny
    parts = 4
    scale_x = -1.0 / math.sqrt(total_x)
    scale_z = -1.0 / math.sqrt(total_z)

    def body(l_ref, w_ref, xt, zt, m_ref, out, rim, made, sems):
        box = Outbox(sems)
        mean = xt[1]

        def along_x(b, acc):
            for k in range(8):
                i = b * 8 + k
                g = w_ref[i]
                made[0, i] = scale_x * (acc + 0.5 * g)
                acc = acc + (g - mean)
            return acc

        acc = xt[0]
        for p in range(parts):
            acc = lax.fori_loop(p * nx // parts // 8, (p + 1) * nx // parts // 8, along_x, acc)
            at = pl.ds(p * nx // parts, nx // parts)
            box.send(made.at[0, at], out.at[0, at])
        rim[:, 6:, :] = jnp.zeros((chunks, 10, LANES), F32)
        for q in range(2):
            for p, part in enumerate(split3(zt[q])):
                rim[:, 3 * q + p, :] = part.astype(F32)
        for p in range(parts):
            at = pl.ds(p * nx // parts, nx // parts)
            here = range(p * chunks // parts, (p + 1) * chunks // parts)
            st = jnp.concatenate([rim[c].T.astype(BF16) for c in here], 0)
            g = l_ref[at].reshape(rows // parts, nz) + dot(st, m_ref[1, LANES : LANES + 16])
            made[1, at] = (scale_z * g).reshape(nx // parts, ny, nz)
            box.send(made.at[1, at], out.at[1, at])
        box.wait()

    shape = (2,) + gw.shape
    return pl.pallas_call(
        body,
        in_specs=[VMEM] * 5,
        out_specs=ANY,
        out_shape=jax.ShapeDtypeStruct(shape, F32),
        scratch_shapes=[
            pltpu.VMEM((chunks, 16, LANES), F32),
            pltpu.VMEM(shape, F32),
            pltpu.SemaphoreType.DMA((16,)),
        ],
        compiler_params=params(),
        name="rebuild",
        cost_estimate=cost(2, nx * ny * nz),
    )(local, gw, x_terms, z_terms, mats)


def swap(axis, up, down):
    n = lax.axis_size(axis)
    before = lax.ppermute(up, axis, [(i, (i + 1) % n) for i in range(n)])
    after = lax.ppermute(down, axis, [((i + 1) % n, i) for i in range(n)])
    return before, after


LEVELS = {
    "gx": [(2, 1, False), (2, 2, False), (4, 2, True)],
    "gz": [(4, 1, False), (2, 4, False), (4, 4, True)],
}
ROUNDS = [(("gx", "gz"), "rest"), (("gx", "gz"), "prepare"), (("gx", "gz"), "flux")]


def shifts(level):
    count, _, mirror = level
    if mirror:
        return [lambda own: count - 1 - 2 * own]
    order = sorted(range(1, count), key=lambda k: min(k, count - k))
    return [lambda own, k=k: (own + k) % count - own for k in order]


def below_tests(level):
    count, _, mirror = level
    if mirror:
        return [count // 2]
    return sorted(range(1, count), key=lambda k: min(k, count - k))


def exchange(axis, terms, level):
    n = lax.axis_size(axis)
    count, stride, _ = level
    parts = []
    for shift in shifts(level):
        pairs = [(i, i + shift((i // stride) % count) * stride) for i in range(n)]
        parts.append(lax.ppermute(terms, axis, pairs))
    return parts


def combine(terms, before, parts, below):
    for mask, part in zip(below, parts):
        before = before + mask * part[0]
        terms = terms + part
    return terms, before


def place(axis, cells):
    n = lax.axis_size(axis)
    mine = lax.axis_index(axis)
    below = []
    for level in LEVELS[axis]:
        own = mine // level[1] % level[0]
        below += [(own >= least).astype(F32) for least in below_tests(level)]
    start = (mine * cells).astype(F32)
    centre = start + (0.5 * (cells - 1) - 0.5 * (n * cells - 1))
    return below, centre, (start + 0.5) * (1.0 / (n * cells))


def below_of(axis, spot, at):
    skip = sum(len(below_tests(level)) for level in LEVELS[axis][:at])
    return [spot[skip + k] for k in range(len(below_tests(LEVELS[axis][at])))]


def line_terms(terms, before, start, total_len):
    mean = terms[0] / total_len
    offset = before - start * terms[0] + terms[1] / total_len
    return jnp.stack([offset, mean])


def body(velocity):
    _, nx, ny, nz = velocity.shape
    size_x = lax.axis_size("gx")
    size_z = lax.axis_size("gz")
    total_x = nx * size_x
    total_z = nz * size_z
    inner_mats = jnp.asarray(z_inner())
    rims = jnp.asarray(z_rims(len(Z_SUMS)))
    sums = jnp.asarray(sum_matrices())

    xu, xd, zu, zd, vel = edges_call(velocity)
    z_halo = (*swap("gz", zu, zd), zd, zu)
    x_halo = swap("gx", xu, xd)
    in_w, in_u, in_v, *in_c = inner_z(vel, inner_mats)
    gu, gw, tx, tz, spot_x, spot_z = slopes_first(vel, in_w, x_halo, z_halo, rims)
    bx = jnp.zeros_like(tx[0])
    bz = jnp.zeros_like(tz[0])

    terms = {"gx": (tx, bx), "gz": (tz, bz)}
    spots = {"gx": spot_x, "gz": spot_z}
    done = {"gx": 0, "gz": 0}
    for axes, filler in ROUNDS:
        parts = {axis: exchange(axis, terms[axis][0], LEVELS[axis][done[axis]]) for axis in axes}
        made = ()
        if filler == "rest":
            made = slopes_rest(vel, in_u, in_v, x_halo, z_halo, rims, gw)
        elif filler == "flux":
            made = divergence(vel, in_c, x_halo)
        elif filler == "prepare":
            made = prepare(in_c, st, rims, (gu, gv, gq), sums)
        if filler:
            parts, made = lax.optimization_barrier((parts, made))
        if filler == "rest":
            gv, gq, st, grad_z = made
        elif filler == "prepare":
            in_c, local, grad_x = made
        elif filler == "flux":
            convect = made
        for axis in axes:
            below = below_of(axis, spots[axis], done[axis])
            terms[axis] = combine(*terms[axis], parts[axis], below)
            done[axis] += 1
    (tx, bx), (tz, bz) = terms["gx"], terms["gz"]
    rebuilt = rebuild(
        local,
        gw,
        line_terms(tx, bx, spot_x[-1], total_x),
        line_terms(tz, bz, spot_z[-1], total_z),
        sums,
        total_x,
        total_z,
    )
    return (grad_x, grad_z, convect, rebuilt)


def solution(mesh):
    spec = P(None, "gx", None, "gz")
    return jax.shard_map(
        body, mesh=mesh, in_specs=(spec,), out_specs=(spec,) * 4, check_vma=False
    )
```

```python
import math

import jax
import jax.numpy as jnp
import numpy as np
from jax import lax
from jax.experimental import pallas as pl
from jax.experimental.pallas import tpu as pltpu
from jax.sharding import PartitionSpec as P

ALPHA = 1.0 / 3.0
COEF_A = 14.0 / 9.0
COEF_B = 1.0 / 9.0
LANES = 128
F32 = jnp.float32
VMEM = pl.BlockSpec(memory_space=pltpu.VMEM)
HBM = pl.BlockSpec(memory_space=pltpu.HBM)
ANY = pl.BlockSpec(memory_space=pl.ANY)
BF16 = jnp.bfloat16

RHO = (-1.0 + math.sqrt(1.0 - 4.0 * ALPHA * ALPHA)) / (2.0 * ALPHA)


def kernel_weights():
    reach = 400
    k = np.arange(-reach, reach + 1)
    green = RHO ** np.abs(k).astype(np.float64) / math.sqrt(1.0 - 4.0 * ALPHA * ALPHA)

    def shifted(s):
        out = np.zeros_like(green)
        if s >= 0:
            out[s:] = green[: len(green) - s]
        else:
            out[:s] = green[-s:]
        return out

    direct = 0.5 * COEF_A * (shifted(-1) - shifted(1)) + 0.25 * COEF_B * (shifted(-2) - shifted(2))
    total = np.concatenate([[0.0], np.cumsum(direct)])
    return {m: total[m + reach] for m in range(-2, 4)}


_W = kernel_weights()
NEAR = _W[1]
TAIL = _W[2] / RHO**2
KAPPA = TAIL * RHO * RHO
TOGETHER = 16
REACH = 96


def h_of(m):
    m = np.asarray(m)
    m = np.where(m <= 0, 1 - m, m)
    return np.where(m == 1, NEAR, TAIL * RHO ** m.astype(np.float64))


def split_np(x):
    hi = x.astype(BF16)
    lo = (x - hi.astype(np.float64)).astype(BF16)
    return hi, lo


def going_up(length):
    j = np.arange(length)
    w = (RHO - 1.0) * RHO ** (length - j).astype(np.float64)
    w[-1] = RHO**2
    return w


def going_down(length):
    return going_up(length)[::-1] * -1.0


def z_inner():
    j = np.arange(LANES)
    inner = h_of(j[None, :] - j[:, None])
    inner[LANES - 1] = 0.0
    hi, lo = split_np(inner)
    return np.stack([hi, lo])


def z_rims(fields):
    j = np.arange(LANES)
    rim = np.stack(
        [
            h_of(j + 1),
            TAIL * RHO ** j.astype(np.float64),
            h_of(LANES - j),
            TAIL * RHO ** (LANES - 1 - j).astype(np.float64),
        ]
    )
    hi, lo = split_np(rim)
    out = np.zeros((fields, LANES, LANES), BF16)
    for f in range(fields):
        out[f, 12 * f : 12 * f + 12] = np.concatenate([hi, hi, lo], 0)
    return out


def sum_matrices():
    j = np.arange(LANES)
    lower = (j[:, None] < j[None, :]) + 0.5 * (j[:, None] == j[None, :])
    ones = np.ones((3, LANES))
    slope = -np.broadcast_to(j, (3, LANES))
    pad = np.zeros((LANES - 6, LANES))
    first = np.concatenate([lower, lower], 0)
    second = np.concatenate([lower, ones, slope, pad], 0)
    return np.stack([first, second]).astype(BF16)


def split2(x):
    hi = x.astype(BF16)
    return hi, (x - hi.astype(F32)).astype(BF16)


def split3(x):
    hi = x.astype(BF16)
    rest = x - hi.astype(F32)
    mid = rest.astype(BF16)
    return hi, mid, (rest - mid.astype(F32)).astype(BF16)


def dot(a, b):
    return lax.dot_general(a, b, (((1,), (0,)), ((), ())), preferred_element_type=F32)


def product(values, name):
    out = values[name[0]]
    for c in name[1:]:
        out = out * values[c]
    return out


COMP = {"u": 0, "v": 1, "w": 2}


X_SUMS = ["u", "v", "w", "uu", "uv", "uw"]
Z_SUMS = ["u", "v", "w", "wu", "wv", "ww"]
CELLS = ["u", "v", "w"]


def z_weights(nz, cut):
    row = lax.broadcasted_iota(jnp.int32, (8, LANES), 0)

    def tiles(powers, factors):
        tile = jnp.zeros((8, LANES), F32)
        for k in range(8):
            tile = jnp.where(row == k, np.float32(powers[k]), tile)
        return [tile * np.float32(f) for f in factors]

    up = going_up(nz)[nz - cut :]
    down = going_down(nz)[:cut]
    ups = tiles(up[:8] / up[0], up[::8])
    ups[-1] = jnp.where(row == 7, np.float32(up[-1]), ups[-1])
    steady = down[8:16] / down[8]
    downs = tiles(steady, [down[8] / RHO**8] + list(down[8::8]))
    downs[0] = jnp.where(row == 0, np.float32(down[0]), downs[0])
    return jnp.concatenate(ups, 0), jnp.concatenate(downs, 0)


def edges_call(velocity):
    _, nx, ny, nz = velocity.shape
    sub = LANES // ny
    chunks = nx // sub
    nq = len(Z_SUMS) + len(CELLS)
    cut_x = min(REACH, nx)
    cut = min(REACH, nz)
    group = 8
    parts = 4
    part = nx // parts

    def body(v_hbm, xu_ref, xd_ref, zu_ref, zd_ref, v_ref, sems):
        copies = [
            pltpu.make_async_copy(
                v_hbm.at[:, pl.ds(p * part, part)], v_ref.at[:, pl.ds(p * part, part)], sems.at[p]
            )
            for p in range(parts)
        ]
        for copy in copies:
            copy.start()
        weight_up, weight_down = z_weights(nz, cut)

        def x_rows(acc, weights, rows):
            for i in rows:
                vals = {c: v_ref[COMP[c], i] for c in CELLS}
                for q, name in enumerate(X_SUMS):
                    term = product(vals, name) * np.float32(weights[i])
                    acc[q] = term if acc[q] is None else acc[q] + term

        ups = [None] * len(X_SUMS)
        downs = [None] * len(X_SUMS)
        rows = {}
        for p in range(parts):
            copies[p].wait()
            for s in range(p * part // sub, (p + 1) * part // sub):
                t = {c: v_ref[COMP[c], s * sub : (s + 1) * sub].reshape(LANES, nz).T for c in CELLS}
                for q, name in enumerate(Z_SUMS):
                    f = product(t, name)
                    up = jnp.sum(f[nz - cut :] * weight_up, axis=0, keepdims=True)
                    down = jnp.sum(f[:cut] * weight_down, axis=0, keepdims=True)
                    rows.setdefault(q, []).append((up, down))
                for q, name in enumerate(CELLS):
                    rows.setdefault(len(Z_SUMS) + q, []).append((t[name][nz - 1 : nz], t[name][0:1]))
                if (s + 1) % group == 0:
                    at = s + 1 - group
                    for q, pairs in rows.items():
                        zu_ref[q, at : at + group] = jnp.concatenate([r[0] for r in pairs], 0)
                        zd_ref[q, at : at + group] = jnp.concatenate([r[1] for r in pairs], 0)
                    rows = {}
            here = range(p * part, (p + 1) * part)
            x_rows(downs, going_down(nx), [i for i in here if i < cut_x])
            x_rows(ups, going_up(nx), [i for i in here if i >= nx - cut_x])
        for q in range(len(X_SUMS)):
            xu_ref[q] = ups[q]
            xd_ref[q] = downs[q]
        for q in range(len(CELLS)):
            xu_ref[len(X_SUMS) + q] = v_ref[q, nx - 1]
            xd_ref[len(X_SUMS) + q] = v_ref[q, 0]

    xs = jax.ShapeDtypeStruct((nq, ny, nz), F32)
    zs = jax.ShapeDtypeStruct((nq, chunks, LANES), F32)
    return pl.pallas_call(
        body,
        in_specs=[HBM],
        out_specs=[VMEM] * 5,
        out_shape=[xs, xs, zs, zs, jax.ShapeDtypeStruct(velocity.shape, F32)],
        scratch_shapes=[pltpu.SemaphoreType.DMA((parts,))],
        compiler_params=params(),
        name="edges",
        cost_estimate=cost(6, nx * ny * nz),
    )(pltpu.with_memory_space_constraint(velocity, pltpu.HBM))


def x_derivatives(read, write, scratch, nx, rims, pieces=1, done=None):
    unroll = 8
    half = nx // 2
    blocks = half // unroll
    fields = range(len(rims))
    grown = [KAPPA * RHO ** -(k + 1) for k in range(unroll)]
    power = [RHO**k for k in range(unroll + 1)]

    def sweep(first):
        def step(b, carry):
            out = []
            lows = (0 if first else half) + b * unroll
            highs = (nx if first else half) - 1 - b * unroll
            for f in fields:
                low, before, here, high, after, there = carry[f]
                _, cell_before, _, cell_after = rims[f]
                for k in range(unroll):
                    i = lows + k
                    part = low if k == 0 else power[k] * low
                    edge = here - before
                    if first:
                        nxt = read(f, i + 1)
                        scratch(f)[i] = part
                    else:
                        if k == unroll - 1:
                            inside = read(f, jnp.minimum(i + 1, nx - 1))
                            nxt = jnp.where(b == blocks - 1, cell_after, inside)
                        else:
                            nxt = read(f, i + 1)
                        write(f, i, scratch(f)[i] + (part + NEAR * (nxt - before)))
                    low = low + grown[k] * edge
                    before, here = here, nxt

                    i = highs - k
                    part = high if k == 0 else power[k] * high
                    edge = after - there
                    if first:
                        nxt = read(f, i - 1)
                        scratch(f)[i] = part
                    else:
                        if k == unroll - 1:
                            inside = read(f, jnp.maximum(i - 1, 0))
                            nxt = jnp.where(b == blocks - 1, cell_before, inside)
                        else:
                            nxt = read(f, i - 1)
                        write(f, i, scratch(f)[i] + (part + NEAR * (after - nxt)))
                    high = high + grown[k] * edge
                    after, there = there, nxt
                out.append((power[unroll] * low, before, here, power[unroll] * high, after, there))
            return tuple(out)

        return step

    carry = tuple(
        (TAIL * sum_before, cell_before, read(f, 0), TAIL * sum_after, cell_after, read(f, nx - 1))
        for f, (sum_before, cell_before, sum_after, cell_after) in enumerate(rims)
    )
    carry = lax.fori_loop(0, blocks, sweep(True), carry)
    for p in range(pieces):
        lo, hi = p * blocks // pieces, (p + 1) * blocks // pieces
        carry = lax.fori_loop(lo, hi, sweep(False), carry)
        if done is not None:
            done(half + lo * unroll, (hi - lo) * unroll)
            done(half - hi * unroll, (hi - lo) * unroll)


def rim_terms(rim, base, field, zl, zr, own_l, own_r):
    cells = [r[6 + field % 3] for r in (zl, own_l, own_r, zr)]
    if field >= 3:
        cells = [c * r[8] for c, r in zip(cells, (zl, own_l, own_r, zr))]
    terms = [cells[1] - cells[0], zl[field], cells[3] - cells[2], zr[field]]
    for q, term in enumerate(terms):
        hi = term.astype(BF16).astype(F32)
        lo = (term - hi).astype(BF16).astype(F32)
        rim[:, base + q, :] = hi
        rim[:, base + 4 + q, :] = lo
        rim[:, base + 8 + q, :] = hi


class Outbox:
    def __init__(self, sems):
        self.sems, self.copies = sems, []

    def send(self, src, dst):
        copy = pltpu.make_async_copy(src, dst, self.sems.at[len(self.copies)])
        copy.start()
        self.copies.append(copy)

    def wait(self):
        for copy in self.copies:
            copy.wait()


def params(mib=8):
    return pltpu.CompilerParams(vmem_limit_bytes=mib * 2**20)


def cost(fields, size):
    return pl.CostEstimate(flops=fields * size * 512, transcendentals=0, bytes_accessed=fields * size * 8)


def inner_z(velocity, inner):
    _, nx, ny, nz = velocity.shape
    rows = nx * ny

    def body(v_ref, m_ref, w_out, u_out, v_out, *c_outs):
        outs = (u_out, v_out, w_out) + c_outs
        keep = lax.broadcasted_iota(jnp.int32, (rows, LANES), 1) < LANES - 1
        both = jnp.concatenate([m_ref[0], m_ref[0]], 0)
        w = v_ref[2].reshape(rows, nz)
        for c in range(6):
            f = v_ref[c % 3].reshape(rows, nz)
            if c >= 3:
                f = f * w
            e = jnp.where(keep, pltpu.roll(f, LANES - 1, 1) - f, 0.0)
            hi, lo = split2(e)
            g = dot(jnp.concatenate([hi, lo], 1), both) + dot(hi, m_ref[1])
            outs[c][...] = g.reshape(nx, ny, nz)

    return pl.pallas_call(
        body,
        in_specs=[VMEM, VMEM],
        out_specs=[VMEM] * 6,
        out_shape=[jax.ShapeDtypeStruct(velocity.shape[1:], F32)] * 6,
        compiler_params=params(),
        name="inner_z",
        cost_estimate=cost(6, nx * ny * nz),
    )(velocity, inner)


def slopes_first(velocity, inner, x_halo, z_halo, rims):
    _, nx, ny, nz = velocity.shape
    sub = LANES // ny
    chunks = nx // sub
    rows = nx * ny

    def body(v_ref, i_ref, xl, xr, zl, zr, own_l, own_r, m_ref, gu, gw, tx, tz, px, pz, scratch, rim):
        rim[:, 12:, :] = jnp.zeros((chunks, 4, LANES), F32)
        rim_terms(rim, 0, 2, zl, zr, own_l, own_r)
        st = jnp.concatenate([rim[c].T.astype(BF16) for c in range(chunks)], 0)
        g = i_ref[...].reshape(rows, nz) + dot(st, m_ref[2, 24:40])
        gw[...] = g.reshape(nx, ny, nz)

        def write_x(_, i, g):
            gu[i] = g

        rims_x = [(xl[0], xl[6], xr[0], xr[6])]
        x_derivatives(lambda _, i: v_ref[0, i], write_x, lambda _: scratch, nx, rims_x)

        zero = jnp.zeros((ny, nz), F32)
        ways = 4

        def add(b, carry):
            out = []
            for k, (total, moment) in enumerate(carry):
                for n in range(2):
                    i = b * 2 * ways + 2 * k + n
                    g = gw[i]
                    total = total + g
                    moment = moment + (i.astype(F32) - 0.5 * (nx - 1)) * g
                out.append((total, moment))
            return tuple(out)

        got = lax.fori_loop(0, nx // (2 * ways), add, ((zero, zero),) * ways)
        bits, centre, start = place("gx", nx)
        total = (got[0][0] + got[1][0]) + (got[2][0] + got[3][0])
        tx[0] = total
        tx[1] = (got[0][1] + got[1][1]) + (got[2][1] + got[3][1]) + centre * total
        for k, value in enumerate([*bits, start]):
            px[k] = jnp.full((ny, nz), value, F32)

        at = lax.broadcasted_iota(jnp.int32, (nz, LANES), 0).astype(F32) - 0.5 * (nz - 1)
        totals, moments = [], []
        for c in range(chunks):
            t = gu[c * sub : (c + 1) * sub].reshape(LANES, nz).T
            totals.append(jnp.sum(t, axis=0, keepdims=True))
            moments.append(jnp.sum(t * at, axis=0, keepdims=True))
        bits, centre, start = place("gz", nz)
        total = jnp.concatenate(totals, 0)
        tz[0] = total
        tz[1] = jnp.concatenate(moments, 0) + centre * total
        for k, value in enumerate([*bits, start]):
            pz[k] = jnp.full((chunks, LANES), value, F32)

    one = jax.ShapeDtypeStruct(velocity.shape[1:], F32)
    sx = jax.ShapeDtypeStruct((2, ny, nz), F32)
    sz = jax.ShapeDtypeStruct((2, chunks, LANES), F32)
    small = [*x_halo, *z_halo, rims]
    steps_x = sum(len(below_tests(level)) for level in LEVELS["gx"])
    steps_z = sum(len(below_tests(level)) for level in LEVELS["gz"])
    px = jax.ShapeDtypeStruct((steps_x + 1, ny, nz), F32)
    pz = jax.ShapeDtypeStruct((steps_z + 1, chunks, LANES), F32)
    outs = [one, one, sx, sz, px, pz]
    return pl.pallas_call(
        body,
        in_specs=[VMEM] * (2 + len(small)),
        out_specs=[VMEM] * len(outs),
        out_shape=outs,
        scratch_shapes=[pltpu.VMEM((nx, ny, nz), F32), pltpu.VMEM((chunks, 16, LANES), F32)],
        compiler_params=params(),
        name="slopes_first",
        cost_estimate=cost(2, nx * ny * nz),
    )(velocity, inner, *small)


def slopes_rest(velocity, inner_u, inner_v, x_halo, z_halo, rims, gw):
    _, nx, ny, nz = velocity.shape
    rows = nx * ny
    parts = 2

    chunks = rows // LANES

    def body(*refs):
        v_ref, iu_ref, iv_ref, xl, xr, zl, zr, own_l, own_r, m_ref, gw_ref = refs[:11]
        gv, gx, st_ref, out, s0, s1, made, rim, flux_rim, sems = refs[11:]
        box = Outbox(sems)
        box.send(gw_ref, out.at[2])
        rim[:, 24:32, :] = jnp.zeros((chunks, 8, LANES), F32)
        for field in (0, 1):
            rim_terms(rim, 12 * field, field, zl, zr, own_l, own_r)
        st = jnp.concatenate([rim[c].T.astype(BF16) for c in range(chunks)], 0)
        for c, i_ref in enumerate((iu_ref, iv_ref)):
            for p in range(parts):
                at = pl.ds(p * nx // parts, nx // parts)
                local = i_ref[at].reshape(rows // parts, nz)
                st_p = st[p * rows // parts : (p + 1) * rows // parts]
                g = local + dot(st_p, m_ref[c, :32])
                made[c, at] = g.reshape(nx // parts, ny, nz)
                box.send(made.at[c, at], out.at[c, at])

        def write(f, i, g):
            (gv, gx)[f][i] = g

        x_derivatives(
            lambda f, i: v_ref[1 + f, i],
            write,
            lambda f: (s0, s1)[f],
            nx,
            [(xl[c], xl[6 + c], xr[c], xr[6 + c]) for c in (1, 2)],
        )
        flux_rim[:, :4, :] = jnp.zeros((chunks, 4, LANES), F32)
        flux_rim[:, 40:, :] = jnp.zeros((chunks, 8, LANES), F32)
        for field in (3, 4, 5):
            rim_terms(flux_rim, 12 * field - 32, field, zl, zr, own_l, own_r)
        for c in range(chunks):
            st_ref[c * LANES : (c + 1) * LANES] = flux_rim[c].T.astype(BF16)
        box.wait()

    one = jax.ShapeDtypeStruct((nx, ny, nz), F32)
    return pl.pallas_call(
        body,
        in_specs=[VMEM] * 11,
        out_specs=[VMEM, VMEM, VMEM, ANY],
        out_shape=[
            one,
            one,
            jax.ShapeDtypeStruct((rows, 48), BF16),
            jax.ShapeDtypeStruct(velocity.shape, F32),
        ],
        scratch_shapes=[
            pltpu.VMEM((nx, ny, nz), F32),
            pltpu.VMEM((nx, ny, nz), F32),
            pltpu.VMEM((2, nx, ny, nz), F32),
            pltpu.VMEM((chunks, 32, LANES), F32),
            pltpu.VMEM((chunks, 48, LANES), F32),
            pltpu.SemaphoreType.DMA((8,)),
        ],
        compiler_params=params(),
        name="slopes_rest",
        cost_estimate=cost(3, nx * ny * nz),
    )(velocity, inner_u, inner_v, *x_halo, *z_halo, rims, gw)


def prepare(inner, st, rims, slopes, sums):
    nx, ny, nz = slopes[0].shape
    rows = nx * ny

    def body(*refs):
        i_refs, g_refs, st_ref, m_ref, t_ref = refs[:3], refs[3:6], *refs[6:9]
        *c_refs, local, gx, sems = refs[9:]
        box = Outbox(sems)
        for c in range(3):
            box.send(g_refs[c], gx.at[c])
        hi, mid, lo = split3(g_refs[0][...].reshape(rows, nz))
        g = dot(jnp.concatenate([hi, mid], 1), t_ref[0]) + dot(lo, t_ref[1, :LANES])
        local[...] = g.reshape(nx, ny, nz)
        for c in range(3):
            g = i_refs[c][...].reshape(rows, nz) + dot(st_ref[...], m_ref[3 + c, 32:80])
            c_refs[c][...] = g.reshape(nx, ny, nz)
        box.wait()

    one = jax.ShapeDtypeStruct((nx, ny, nz), F32)
    *parts, local, gx = pl.pallas_call(
        body,
        in_specs=[VMEM] * 9,
        out_specs=[VMEM] * 4 + [ANY],
        out_shape=[one] * 4 + [jax.ShapeDtypeStruct((3, nx, ny, nz), F32)],
        scratch_shapes=[pltpu.SemaphoreType.DMA((4,))],
        compiler_params=params(),
        name="prepare",
        cost_estimate=cost(3, nx * ny * nz),
    )(*inner, *slopes, st, rims, sums)
    return parts, local, gx


def divergence(velocity, along_z, x_halo):
    _, nx, ny, nz = velocity.shape
    comps = range(3)

    def body(v_ref, xl, xr, *rest):
        z_refs = rest[:3]
        out, s0, s1, s2, m0, m1, m2, sems = rest[3:]
        made = (m0, m1, m2)
        box = Outbox(sems)

        def write(c, i, g):
            made[c][i] = z_refs[c][i] + g

        def done(start, size):
            at = pl.ds(start, size)
            for c in comps:
                box.send(made[c].at[at], out.at[c, at])

        x_derivatives(
            lambda c, i: v_ref[0, i] * v_ref[c, i],
            write,
            lambda c: (s0, s1, s2)[c],
            nx,
            [(xl[3 + c], xl[6] * xl[6 + c], xr[3 + c], xr[6] * xr[6 + c]) for c in comps],
            4,
            done,
        )
        box.wait()

    return pl.pallas_call(
        body,
        in_specs=[VMEM] * 6,
        out_specs=ANY,
        out_shape=jax.ShapeDtypeStruct(velocity.shape, F32),
        scratch_shapes=[pltpu.VMEM((nx, ny, nz), F32)] * 6 + [pltpu.SemaphoreType.DMA((32,))],
        compiler_params=params(12),
        name="divergence",
        cost_estimate=cost(6, nx * ny * nz),
    )(velocity, *x_halo, *along_z)


def rebuild(local, gw, x_terms, z_terms, mats, total_x, total_z):
    nx, ny, nz = gw.shape
    sub = LANES // ny
    chunks = nx // sub
    rows = nx * ny
    parts = 8
    scale_x = -1.0 / math.sqrt(total_x)
    scale_z = -1.0 / math.sqrt(total_z)

    def body(l_ref, w_ref, xt, zt, m_ref, out, rim, made, sems):
        box = Outbox(sems)
        mean = xt[1]

        def along_x(b, acc):
            for k in range(8):
                i = b * 8 + k
                g = w_ref[i]
                made[0, i] = scale_x * (acc + 0.5 * g)
                acc = acc + (g - mean)
            return acc

        acc = xt[0]
        for p in range(parts):
            acc = lax.fori_loop(p * nx // parts // 8, (p + 1) * nx // parts // 8, along_x, acc)
            at = pl.ds(p * nx // parts, nx // parts)
            box.send(made.at[0, at], out.at[0, at])
        rim[:, 6:, :] = jnp.zeros((chunks, 10, LANES), F32)
        for q in range(2):
            for p, part in enumerate(split3(zt[q])):
                rim[:, 3 * q + p, :] = part.astype(F32)
        for p in range(parts):
            at = pl.ds(p * nx // parts, nx // parts)
            here = range(p * chunks // parts, (p + 1) * chunks // parts)
            st = jnp.concatenate([rim[c].T.astype(BF16) for c in here], 0)
            g = l_ref[at].reshape(rows // parts, nz) + dot(st, m_ref[1, LANES : LANES + 16])
            made[1, at] = (scale_z * g).reshape(nx // parts, ny, nz)
            box.send(made.at[1, at], out.at[1, at])
        box.wait()

    shape = (2,) + gw.shape
    return pl.pallas_call(
        body,
        in_specs=[VMEM] * 5,
        out_specs=ANY,
        out_shape=jax.ShapeDtypeStruct(shape, F32),
        scratch_shapes=[
            pltpu.VMEM((chunks, 16, LANES), F32),
            pltpu.VMEM(shape, F32),
            pltpu.SemaphoreType.DMA((16,)),
        ],
        compiler_params=params(),
        name="rebuild",
        cost_estimate=cost(2, nx * ny * nz),
    )(local, gw, x_terms, z_terms, mats)


def swap(axis, up, down):
    n = lax.axis_size(axis)
    before = lax.ppermute(up, axis, [(i, (i + 1) % n) for i in range(n)])
    after = lax.ppermute(down, axis, [((i + 1) % n, i) for i in range(n)])
    return before, after


LEVELS = {
    "gx": [(2, 1, False), (2, 2, False), (4, 2, True)],
    "gz": [(4, 1, False), (2, 4, False), (4, 4, True)],
}
ROUNDS = [(("gx", "gz"), "rest"), (("gx", "gz"), "prepare"), (("gx", "gz"), "flux")]


def shifts(level):
    count, _, mirror = level
    if mirror:
        return [lambda own: count - 1 - 2 * own]
    order = sorted(range(1, count), key=lambda k: min(k, count - k))
    return [lambda own, k=k: (own + k) % count - own for k in order]


def below_tests(level):
    count, _, mirror = level
    if mirror:
        return [count // 2]
    return sorted(range(1, count), key=lambda k: min(k, count - k))


def exchange(axis, terms, level):
    n = lax.axis_size(axis)
    count, stride, _ = level
    parts = []
    for shift in shifts(level):
        pairs = [(i, i + shift((i // stride) % count) * stride) for i in range(n)]
        parts.append(lax.ppermute(terms, axis, pairs))
    return parts


def combine(terms, before, parts, below):
    for mask, part in zip(below, parts):
        before = before + mask * part[0]
        terms = terms + part
    return terms, before


def place(axis, cells):
    n = lax.axis_size(axis)
    mine = lax.axis_index(axis)
    below = []
    for level in LEVELS[axis]:
        own = mine // level[1] % level[0]
        below += [(own >= least).astype(F32) for least in below_tests(level)]
    start = (mine * cells).astype(F32)
    centre = start + (0.5 * (cells - 1) - 0.5 * (n * cells - 1))
    return below, centre, (start + 0.5) * (1.0 / (n * cells))


def below_of(axis, spot, at):
    skip = sum(len(below_tests(level)) for level in LEVELS[axis][:at])
    return [spot[skip + k] for k in range(len(below_tests(LEVELS[axis][at])))]


def line_terms(terms, before, start, total_len):
    mean = terms[0] / total_len
    offset = before - start * terms[0] + terms[1] / total_len
    return jnp.stack([offset, mean])


def body(velocity):
    _, nx, ny, nz = velocity.shape
    size_x = lax.axis_size("gx")
    size_z = lax.axis_size("gz")
    total_x = nx * size_x
    total_z = nz * size_z
    inner_mats = jnp.asarray(z_inner())
    rims = jnp.asarray(z_rims(len(Z_SUMS)))
    sums = jnp.asarray(sum_matrices())

    xu, xd, zu, zd, vel = edges_call(velocity)
    z_halo = (*swap("gz", zu, zd), zd, zu)
    x_halo = swap("gx", xu, xd)
    in_w, in_u, in_v, *in_c = inner_z(vel, inner_mats)
    gu, gw, tx, tz, spot_x, spot_z = slopes_first(vel, in_w, x_halo, z_halo, rims)
    bx = jnp.zeros_like(tx[0])
    bz = jnp.zeros_like(tz[0])

    terms = {"gx": (tx, bx), "gz": (tz, bz)}
    spots = {"gx": spot_x, "gz": spot_z}
    done = {"gx": 0, "gz": 0}
    for axes, filler in ROUNDS:
        parts = {axis: exchange(axis, terms[axis][0], LEVELS[axis][done[axis]]) for axis in axes}
        made = ()
        if filler == "rest":
            made = slopes_rest(vel, in_u, in_v, x_halo, z_halo, rims, gw)
        elif filler == "flux":
            made = divergence(vel, in_c, x_halo)
        elif filler == "prepare":
            made = prepare(in_c, st, rims, (gu, gv, gq), sums)
        if filler:
            parts, made = lax.optimization_barrier((parts, made))
        if filler == "rest":
            gv, gq, st, grad_z = made
        elif filler == "prepare":
            in_c, local, grad_x = made
        elif filler == "flux":
            convect = made
        for axis in axes:
            below = below_of(axis, spots[axis], done[axis])
            terms[axis] = combine(*terms[axis], parts[axis], below)
            done[axis] += 1
    (tx, bx), (tz, bz) = terms["gx"], terms["gz"]
    rebuilt = rebuild(
        local,
        gw,
        line_terms(tx, bx, spot_x[-1], total_x),
        line_terms(tz, bz, spot_z[-1], total_z),
        sums,
        total_x,
        total_z,
    )
    return (grad_x, grad_z, convect, rebuilt)


def solution(mesh):
    spec = P(None, "gx", None, "gz")
    return jax.shard_map(
        body, mesh=mesh, in_specs=(spec,), out_specs=(spec,) * 4, check_vma=False
    )
```
